32 devices in a mesh: tile: 8 (over z, y), ka: 4 (over x, core).
Axes of the slice: x: 2, y: 2, z: 4, core: 2. Of those that a mesh axis runs over, the one named last changes fastest.
Arguments:
- integrals: bfloat16 [640, 48, 640], P('tile', 'ka'), may hold values from -0.03125 to 0.03125
- amplitudes: bfloat16 [48, 640, 8, 640], P('ka', 'tile'), may hold values from -24 to 24
- virt_energy: float32 [640], replicated, may hold values from 0.5 to 3
- pair_energy: float32 [8], replicated, may hold values from -6 to -1
Outputs:
- update: bfloat16 [8, 640, 640], P('ka', 'tile')
The draws below stay inside these ranges and needn't reach their ends.
All inputs are finite; a program needn't handle non-finite values.
Results may differ from the reference program's by a relative error of at most 0.001.
Values may be sent and summed in bfloat16 or wider, within the bound.
No kernel may reach another device: no remote copies, remote signals or barrier semaphores. Data moves between devices by JAX's collectives and lax.ppermute only.
A program may use at most 128 MiB of HBM per device.

```python
import jax
import jax.numpy as jnp

V = 640
O = 48
NJ = 8


def levels(rng, extent, shards, low, high):
    loudness = 1.0
    for position, parts in shards:
        heights = jax.random.uniform(jax.random.fold_in(jax.random.fold_in(rng, 6), position), (parts,), jnp.float32, low / len(shards), high / len(shards))
        loudness = loudness * jnp.repeat(jnp.exp(heights), extent[position] // parts).reshape((-1,) + (1,) * (len(extent) - 1 - position))
    return loudness


def normal_values(own_key, extent, deviation, limit, shards=(), held_as=jnp.bfloat16):
    entries = deviation * jax.random.normal(own_key, extent, jnp.float32)
    if shards:
        entries = entries * levels(own_key, extent, shards, -0.22, 0.18)
    return jnp.clip(entries, -limit, limit).astype(held_as)


def setup_inputs(seed: int = 0) -> dict:
    seeds = jax.random.split(jax.random.key(seed), 5)
    integrals = normal_values(seeds[0], (V, O, V), (O * V) ** -0.5, 0.03125, ((0, 8), (1, 4)))
    amplitudes = normal_values(seeds[1], (O, V, NJ, V), 4.0, 24.0, ((0, 4), (1, 8)))
    virt_energy = jnp.clip(jax.random.uniform(seeds[2], (V,), jnp.float32, 0.5, 3.0), 0.5, 3.0)
    pair_energy = jnp.clip(jax.random.uniform(seeds[3], (NJ,), jnp.float32, -6.0, -1.0), -6.0, -1.0)
    return dict(integrals=integrals, amplitudes=amplitudes, virt_energy=virt_energy, pair_energy=pair_energy)


def reference(integrals, amplitudes, virt_energy, pair_energy):
    lhs_matrix = jnp.transpose(integrals, (1, 0, 2)).reshape(O * V, V)
    rhs_matrix = amplitudes.reshape(O * V, NJ * V)
    summed = jnp.dot(lhs_matrix.T, rhs_matrix, preferred_element_type=jnp.float32)
    summed = jnp.transpose(summed.reshape(V, NJ, V), (1, 0, 2))
    denominator = virt_energy[None, :, None] + virt_energy[None, None, :] - pair_energy[:, None, None]
    return (summed / denominator).astype(jnp.bfloat16)
```

```python
import jax
import jax.numpy as jnp
from jax import lax
from jax.sharding import PartitionSpec as P


def trade(parts, axis, bit, dim, wire):
    size = lax.axis_size(axis)
    mine = (lax.axis_index(axis) // bit) % 2
    keep = lax.dynamic_index_in_dim(parts, mine, dim, keepdims=False)
    away = lax.dynamic_index_in_dim(parts, 1 - mine, dim, keepdims=False)
    pairs = [(i, i ^ bit) for i in range(size)]
    got = lax.ppermute(away.astype(wire), axis, pairs)
    return keep + got.astype(jnp.float32)


def bits_of(size):
    return [1 << i for i in range(size.bit_length() - 1)]


def per_device(integrals, amplitudes, virt_energy, pair_energy):
    tile_size, ka_size = lax.axis_size("tile"), lax.axis_size("ka")
    summed = jnp.einsum("cka,kcjb->jab", integrals, amplitudes, preferred_element_type=jnp.float32)
    pairs, virt, cols = summed.shape
    own_pairs, own_rows = pairs // ka_size, virt // tile_size
    ka_bits, tile_bits = bits_of(ka_size), bits_of(tile_size)
    grid = summed.reshape([2] * len(ka_bits) + [own_pairs] + [2] * len(tile_bits) + [own_rows, cols])

    def reduce(grid, order):
        left = {("ka", b): i for i, b in enumerate(reversed(ka_bits))}
        left |= {("tile", b): len(ka_bits) + 1 + i for i, b in enumerate(reversed(tile_bits))}
        for step in order:
            axis, bit, wire = step
            dim = left.pop((axis, bit))
            left = {k: d - (d > dim) for k, d in left.items()}
            grid = trade(grid, axis, bit, dim, wire)
        return grid

    f16, f32 = jnp.float16, jnp.float32
    first = [("ka", ka_bits[0], f32)]
    last = [("tile", b, f32) for b in tile_bits[1:]]
    one = [("ka", b, f16) for b in ka_bits[1:]]
    two = [("tile", b, f16) for b in tile_bits[:1]]
    half = own_pairs // 2
    pair_dim = len(ka_bits)
    a = lax.slice_in_dim(grid, 0, half, axis=pair_dim)
    b = lax.slice_in_dim(grid, half, own_pairs, axis=pair_dim)
    reduced = jnp.concatenate([reduce(a, first + one + two + last), reduce(b, first + two + one + last)], 0)
    tile_pos = lax.axis_index("tile")
    ka_pos = lax.axis_index("ka")
    own_virt = lax.dynamic_slice_in_dim(virt_energy, tile_pos * own_rows, own_rows, 0)
    own_e = lax.dynamic_slice_in_dim(pair_energy, ka_pos * own_pairs, own_pairs, 0)
    denominator = own_virt[None, :, None] + virt_energy[None, None, :] - own_e[:, None, None]
    return (reduced / denominator).astype(jnp.bfloat16)


def solution(mesh):
    in_specs = (P("tile", "ka", None), P("ka", "tile", None, None), P(), P())
    out_specs = P("ka", "tile", None)
    return jax.shard_map(
        per_device, mesh=mesh, in_specs=in_specs, out_specs=out_specs, check_vma=False
    )
```

```python
import functools

import jax
import jax.numpy as jnp
from jax import lax
from jax.experimental import pallas as pl
from jax.experimental.pallas import tpu as pltpu
from jax.sharding import PartitionSpec as P

F32, BF16 = jnp.float32, jnp.bfloat16
SPAN, BASE = 248.0, 124.0
EDGE = 16
PAD = 16
FAR = pl.BlockSpec(memory_space=pltpu.HBM)
WHOLE = pl.BlockSpec(memory_space=pltpu.VMEM)
SCALAR = pl.BlockSpec(memory_space=pltpu.SMEM)


def shape(dims, dtype):
    return jax.ShapeDtypeStruct(tuple(dims), dtype)


def encode(out_ref, value):
    rows, cols = value.shape
    tall = value.reshape(rows // 8, 8, cols)
    size = jnp.abs(tall)
    top = jnp.maximum(jnp.max(size, axis=0) * 1.01, 1e-30).astype(BF16)
    factor = SPAN / top.astype(F32)
    code = jnp.exp2(size * factor[None] - BASE)
    code = jnp.where(tall < 0, -code, code)
    out_ref[pl.ds(0, rows), :] = code.reshape(rows, cols).astype(BF16)
    out_ref[pl.ds(rows, PAD), :] = jnp.concatenate([top, top], 0)


def decode(ref, first, rows):
    total, cols = ref.shape[0] - PAD, ref.shape[1]
    factor = ref[pl.ds(total, PAD), :].astype(F32)[:8] * (1.0 / SPAN)
    code = ref[pl.ds(first, rows), :].astype(F32).reshape(rows // 8, 8, cols)
    size = (jnp.log2(jnp.abs(code)) + BASE) * factor[None]
    return jnp.where(code < 0, -size, size).reshape(rows, cols)


def call(kernel, outs, *args, specs=None, room=12, scratch=(), alias=None, after=()):
    specs = list(specs or [WHOLE] * len(args))
    count = len(after)

    def body(*refs):
        kernel(*refs[count:])

    return pl.pallas_call(
        body,
        in_specs=[pl.BlockSpec(memory_space=pl.ANY)] * count + specs,
        out_specs=[WHOLE] * len(outs),
        out_shape=outs,
        scratch_shapes=scratch,
        input_output_aliases={i + count: o for i, o in (alias or {}).items()},
        compiler_params=pltpu.CompilerParams(vmem_limit_bytes=room << 20),
        cost_estimate=pl.CostEstimate(
            flops=1000, bytes_accessed=1000, transcendentals=0
        ),
    )(*after, *args)


def front_kernel(place, wide, amp, turned, out, flat, held, sem, *, block, unit, own_rows, tiles_y, tiles_z):
    depth, pairs, cols = amp.shape
    copies = [
        pltpu.make_async_copy(amp.at[pl.ds(at, block)], held.at[pl.ds(at, block)], sem.at[at // block])
        for at in range(0, depth, block)
    ]
    for copy in copies:
        copy.start()
    t = wide[...].T
    bulk = own_rows - EDGE
    for y in range(tiles_y):
        for z in range(tiles_z):
            at = (z * tiles_y + y) * own_rows
            turned[pl.ds((y * tiles_z + z) * bulk, bulk), :] = t[at : at + bulk]
            edge = tiles_y * tiles_z * bulk + (z * tiles_y + y) * EDGE
            turned[pl.ds(edge, EDGE), :] = t[at + bulk : at + own_rows]
    n = unit * pairs
    r = lax.broadcasted_iota(jnp.int32, (n, n), 0)
    c = lax.broadcasted_iota(jnp.int32, (n, n), 1)
    perm = (c == (r % unit) * pairs + r // unit).astype(F32).astype(BF16)
    for at in range(0, depth, unit):
        if at % block == 0:
            copies[at // block].wait()
        part = held[at : at + unit].reshape(n, cols)
        moved = jnp.dot(perm, part, preferred_element_type=F32).astype(BF16)
        for j in range(pairs):
            flat[j, at : at + unit, :] = moved[j * unit : (j + 1) * unit]
    x, core = place[0], place[1]
    rows = tiles_y * tiles_z * bulk
    out[...] = jnp.dot(
        turned[pl.ds(0, rows), :], flat[4 * (1 - x) + 2 * (1 - core)], preferred_element_type=F32
    )


def product_kernel(place, turned, flat, *outs, jobs, bulk, tiles_y, tiles_z):
    x, core, y = place[0], place[1], place[2]
    rows = tiles_z * bulk

    def dot(at, height, plane):
        return jnp.dot(turned[pl.ds(at, height), :], flat[plane], preferred_element_type=F32)

    for out, (who, part) in zip(outs[:-1], jobs):
        pair = 2 * (core if who == "own" else 1 - core)
        if part == "a_away":
            out[...] = dot(0, 2 * rows, 4 * (1 - x) + pair)
        elif part == "a_home":
            out[...] = dot(0, 2 * rows, 4 * x + pair)
        elif part in ("b_away", "b_home"):
            side = y if part == "b_home" else 1 - y
            for xx in range(2):
                out[pl.ds(xx * rows, rows), :] = dot(pl.multiple_of(side * rows, 16), rows, 4 * xx + pair + 1)
        else:
            for xx in range(2):
                for i in range(2):
                    got = dot(2 * rows, tiles_y * tiles_z * EDGE, 4 * xx + pair + i)
                    for zz in range(tiles_z):
                        for yy in range(tiles_y):
                            at = (((zz * 2 + xx) * tiles_y + yy) * 2 + i) * EDGE
                            out[pl.ds(at, EDGE), :] = got[(zz * tiles_y + yy) * EDGE :][:EDGE]


def first_kernel(own, core, out):
    encode(out, own[...] + core[...])


def spread_kernel(place, own, core, keep, *outs, rows, count):
    z = place[3]

    def total(to):
        at = pl.ds(pl.multiple_of(to * rows, 16), rows)
        return own[at, :] + core[at, :]

    for hop in range(1, count):
        encode(outs[hop - 1], total(z ^ hop))
    keep[...] = total(z)


def mid_kernel(place, own, core, got, keep, out, *, which, rows):
    home = place[which]

    def total(half):
        at = pl.multiple_of(half * rows, 16)
        return own[pl.ds(at, rows), :] + core[pl.ds(at, rows), :] + decode(got, at, rows)

    encode(out, total(1 - home))
    keep[...] = total(home)


def halve_kernel(place, own, *refs, which, rows):
    *gots, keep, out = refs
    home = place[which]

    def total(half):
        at = pl.multiple_of(half * rows, 16)
        value = own[pl.ds(at, rows), :]
        for got in gots:
            value = value + decode(got, at, rows)
        return value

    encode(out, total(1 - home))
    keep[...] = total(home)


def line_kernel(place, keep_a, got_a, keep_b, got_b, own, *outs, rows, count):
    z = place[3]

    def total(to):
        start = pl.multiple_of(to * rows, 16)
        at = pl.ds(start, rows)
        first = keep_a[at, :] + decode(got_a, start, rows)
        second = keep_b[at, :] + decode(got_b, start, rows)
        return jnp.concatenate([first, second], 0)

    for hop in range(1, count):
        encode(outs[hop - 1], total(z ^ hop))
    own[...] = total(z)


def last_kernel(own, keep_c, got_c, *refs):
    gots, (row_e, col_e, pair_e, out) = refs[:-4], refs[-4:]
    value = own[...]
    for got in gots:
        value = value + decode(got, 0, own.shape[0])
    edge = keep_c[...] + decode(got_c, 0, keep_c.shape[0])
    bulk = out.shape[1] - EDGE
    for i in range(out.shape[0]):
        denominator = row_e[...] + col_e[...] - pair_e[i]
        rows = jnp.concatenate([value[i * bulk : (i + 1) * bulk], edge[i * EDGE : (i + 1) * EDGE]], 0)
        out[i] = (rows / denominator).astype(BF16)


def swap(value, axis, bit):
    return lax.ppermute(value, axis, [(i, i ^ bit) for i in range(lax.axis_size(axis))])


def on_chip_plan(integrals, amplitudes, virt_energy, pair_energy):
    tile_size, ka_size = lax.axis_size("tile"), lax.axis_size("ka")
    tile_pos, ka_pos = lax.axis_index("tile"), lax.axis_index("ka")
    k, c, pairs, cols = amplitudes.shape
    depth, virt = k * c, integrals.shape[2]
    own_pairs, own_rows = pairs // ka_size, virt // tile_size
    tiles_y, tiles_z = 2, tile_size // 2
    bulk = own_rows - EDGE
    rows = bulk * tiles_z
    edges = EDGE * tiles_y * own_pairs * 2
    place = jnp.stack([ka_pos // 2, ka_pos % 2, tile_pos % 2, tile_pos // 2]).astype(jnp.int32)
    wide = integrals.transpose(1, 0, 2).reshape(depth, virt)

    def full(height):
        return shape((height, cols), F32)

    def coded(height):
        return shape((height + PAD, cols), BF16)

    block = 160
    held = pltpu.VMEM((pairs, depth, cols), BF16)
    turned, c_a, flat = call(
        functools.partial(
            front_kernel, block=block, unit=32, own_rows=own_rows, tiles_y=tiles_y, tiles_z=tiles_z
        ),
        [pltpu.VMEM((virt, depth), BF16), full(2 * rows), held],
        place, wide, amplitudes.reshape(depth, pairs, cols), specs=[SCALAR, WHOLE, FAR], room=40,
        scratch=[pltpu.VMEM((depth, pairs, cols), BF16), pltpu.SemaphoreType.DMA((depth // block,))],
    )

    def products(flat, *jobs, after=()):
        heights = {"a": 2 * rows, "b": 2 * rows, "c": tiles_z * edges}
        return call(
            functools.partial(product_kernel, jobs=jobs, bulk=bulk, tiles_y=tiles_y, tiles_z=tiles_z),
            [full(heights[part[0]]) for _, part in jobs] + [held], place, turned, flat,
            specs=[SCALAR, WHOLE, WHOLE], alias={2: len(jobs)}, after=after,
        )

    g_a = swap(c_a, "ka", 1)
    c_b, c_c, flat = products(flat, ("core", "b_away"), ("core", "c"))
    g_b, g_c = swap(c_b, "ka", 1), swap(c_c, "ka", 1)
    c_ah, c_bh, flat = products(flat, ("core", "a_home"), ("core", "b_home"))
    g_ah, g_bh = swap(c_ah, "ka", 1), swap(c_bh, "ka", 1)
    o_a, o_b, o_c, o_ah, o_bh, flat = products(
        flat, ("own", "a_away"), ("own", "b_away"), ("own", "c"), ("own", "a_home"), ("own", "b_home")
    )
    (send_a,) = call(first_kernel, [coded(2 * rows)], o_a, g_a)
    got_a = swap(send_a, "ka", 2)
    (send_b,) = call(first_kernel, [coded(2 * rows)], o_b, g_b, after=[send_a])
    got_b = swap(send_b, "tile", 1)
    keep_c, *sends = call(
        functools.partial(spread_kernel, rows=edges, count=tiles_z),
        [full(edges)] + [coded(edges)] * (tiles_z - 1), place, o_c, g_c,
        specs=[SCALAR, WHOLE, WHOLE], after=[send_b],
    )
    gots_c = [swap(s, "tile", 2 * hop) for hop, s in enumerate(sends, 1)]

    mid = functools.partial(mid_kernel, rows=rows)
    specs = [SCALAR, WHOLE, WHOLE, WHOLE]
    keep_a, send_a = call(
        functools.partial(mid, which=2), [full(rows), coded(rows)], place, o_ah, g_ah, got_a, specs=specs
    )
    got_a = swap(send_a, "tile", 1)
    keep_c, send_c = call(
        functools.partial(halve_kernel, which=0, rows=edges // 2), [full(edges // 2), coded(edges // 2)],
        place, keep_c, *gots_c, specs=[SCALAR] + [WHOLE] * tiles_z, after=[keep_a],
    )
    got_c = swap(send_c, "ka", 2)
    keep_b, send_b = call(
        functools.partial(mid, which=0), [full(rows), coded(rows)], place, o_bh, g_bh, got_b,
        specs=specs, after=[send_c],
    )
    got_b = swap(send_b, "ka", 2)

    height = own_pairs * bulk
    own, *sends = call(
        functools.partial(line_kernel, rows=bulk, count=tiles_z),
        [full(height)] + [coded(height)] * (tiles_z - 1), place, keep_a, got_a, keep_b, got_b,
        specs=[SCALAR] + [WHOLE] * 4,
    )
    gots = [swap(s, "tile", 2 * hop) for hop, s in enumerate(sends, 1)]
    keep_c, send_c = call(
        functools.partial(halve_kernel, which=2, rows=edges // 4), [full(edges // 4), coded(edges // 4)],
        place, keep_c, got_c, specs=[SCALAR, WHOLE, WHOLE], after=[own],
    )
    got_c = swap(send_c, "tile", 1)
    own_virt = lax.dynamic_slice_in_dim(virt_energy, tile_pos * own_rows, own_rows, 0)
    own_e = lax.dynamic_slice_in_dim(pair_energy, ka_pos * own_pairs, own_pairs, 0)
    (out,) = call(
        last_kernel, [shape((own_pairs, own_rows, cols), BF16)],
        own, keep_c, got_c, *gots, own_virt[:, None], virt_energy[None, :], own_e,
        specs=[WHOLE] * (3 + len(gots) + 2) + [SCALAR],
    )
    return out


def trade(parts, axis, bit, dim, wire):
    mine = (lax.axis_index(axis) // bit) % 2
    keep = lax.dynamic_index_in_dim(parts, mine, dim, keepdims=False)
    away = lax.dynamic_index_in_dim(parts, 1 - mine, dim, keepdims=False)
    got = swap(away.astype(wire), axis, bit)
    return keep + got.astype(F32)


def bits_of(size):
    return [1 << i for i in range(size.bit_length() - 1)]


def any_plan(integrals, amplitudes, virt_energy, pair_energy):
    tile_size, ka_size = lax.axis_size("tile"), lax.axis_size("ka")
    summed = jnp.einsum("cka,kcjb->jab", integrals, amplitudes, preferred_element_type=F32)
    pairs, virt, cols = summed.shape
    own_pairs, own_rows = pairs // ka_size, virt // tile_size
    ka_bits, tile_bits = bits_of(ka_size), bits_of(tile_size)
    grid = summed.reshape([2] * len(ka_bits) + [own_pairs] + [2] * len(tile_bits) + [own_rows, cols])
    for i, bit in enumerate(ka_bits):
        grid = trade(grid, "ka", bit, len(ka_bits) - 1 - i, F32)
    for i, bit in enumerate(tile_bits):
        grid = trade(grid, "tile", bit, len(tile_bits) - i, F32)
    tile_pos, ka_pos = lax.axis_index("tile"), lax.axis_index("ka")
    own_virt = lax.dynamic_slice_in_dim(virt_energy, tile_pos * own_rows, own_rows, 0)
    own_e = lax.dynamic_slice_in_dim(pair_energy, ka_pos * own_pairs, own_pairs, 0)
    denominator = own_virt[None, :, None] + virt_energy[None, None, :] - own_e[:, None, None]
    return (grid / denominator).astype(BF16)


def solution(mesh):
    fits = mesh.shape["ka"] == 4 and mesh.shape["tile"] == 8

    def per_device(integrals, amplitudes, virt_energy, pair_energy):
        own_rows = integrals.shape[2] // lax.axis_size("tile")
        depth = amplitudes.shape[0] * amplitudes.shape[1]
        plain = fits and own_rows % 16 == 0 and depth % 160 == 0 and amplitudes.shape[2] == 8
        plan = on_chip_plan if plain else any_plan
        return plan(integrals, amplitudes, virt_energy, pair_energy)

    in_specs = (P("tile", "ka", None), P("ka", "tile", None, None), P(), P())
    out_specs = P("ka", "tile", None)
    return jax.shard_map(
        per_device, mesh=mesh, in_specs=in_specs, out_specs=out_specs, check_vma=False
    )
```

```python
import functools

import jax
import jax.numpy as jnp
from jax import lax
from jax.experimental import pallas as pl
from jax.experimental.pallas import tpu as pltpu
from jax.sharding import PartitionSpec as P

F32, BF16 = jnp.float32, jnp.bfloat16
SPAN, BASE = 248.0, 124.0
EDGE = 16
LONG = 1 << 35
PAD = 8
FAR = pl.BlockSpec(memory_space=pltpu.HBM)
WHOLE = pl.BlockSpec(memory_space=pltpu.VMEM)
SCALAR = pl.BlockSpec(memory_space=pltpu.SMEM)


def shape(dims, dtype):
    return jax.ShapeDtypeStruct(tuple(dims), dtype)


def encode(out_ref, value):
    rows, cols = value.shape
    tall = value.reshape(rows // 8, 8, cols)
    size = jnp.abs(tall)
    top = jnp.maximum(jnp.max(size, axis=0) * 1.01, 1e-30).astype(BF16)
    factor = SPAN / top.astype(F32)
    code = jnp.exp2(size * factor[None] - BASE)
    code = jnp.where(tall < 0, -code, code)
    out_ref[pl.ds(0, rows), :] = code.reshape(rows, cols).astype(BF16)
    out_ref[pl.ds(rows, PAD), :] = top


def decode(ref, first, rows):
    total, cols = ref.shape[0] - PAD, ref.shape[1]
    factor = ref[pl.ds(total, PAD), :].astype(F32) * (1.0 / SPAN)
    code = ref[pl.ds(first, rows), :].astype(F32).reshape(rows // 8, 8, cols)
    size = (jnp.log2(jnp.abs(code)) + BASE) * factor[None]
    return jnp.where(code < 0, -size, size).reshape(rows, cols)


def call(kernel, outs, *args, specs=None, room=12, scratch=(), alias=None, after=(), work=1000, out_specs=None):
    specs = list(specs or [WHOLE] * len(args))
    count = len(after)

    def body(*refs):
        kernel(*refs[count:])

    return pl.pallas_call(
        body,
        in_specs=[pl.BlockSpec(memory_space=pl.ANY)] * count + specs,
        out_specs=out_specs or [WHOLE] * len(outs),
        out_shape=outs,
        scratch_shapes=scratch,
        input_output_aliases={i + count: o for i, o in (alias or {}).items()},
        compiler_params=pltpu.CompilerParams(vmem_limit_bytes=room << 20),
        cost_estimate=pl.CostEstimate(
            flops=work, bytes_accessed=1000, transcendentals=0
        ),
    )(*after, *args)


def home_planes(place):
    x, core = place[0], place[1]
    return 4 * x + 2 * core, 2 * core + 1, 4 + 2 * core + 1


def front_kernel(place, wide, amp, turned, out, flat, far, held, sem, far_sem, *, block, unit, own_rows, tiles_y, tiles_z):
    depth, pairs, cols = amp.shape
    copies = [
        pltpu.make_async_copy(amp.at[pl.ds(at, block)], held.at[pl.ds(at, block)], sem.at[at // block])
        for at in range(0, depth, block)
    ]
    for copy in copies:
        copy.start()
    t = wide[...].T
    bulk = own_rows - EDGE
    for y in range(tiles_y):
        for z in range(tiles_z):
            at = (z * tiles_y + y) * own_rows
            turned[pl.ds((y * tiles_z + z) * bulk, bulk), :] = t[at : at + bulk]
            edge = tiles_y * tiles_z * bulk + (z * tiles_y + y) * EDGE
            turned[pl.ds(edge, EDGE), :] = t[at + bulk : at + own_rows]
    leaving = []
    n = unit * pairs
    r = lax.broadcasted_iota(jnp.int32, (n, n), 0)
    c = lax.broadcasted_iota(jnp.int32, (n, n), 1)
    perm = (c == (r % unit) * pairs + r // unit).astype(F32).astype(BF16)
    for at in range(0, depth, unit):
        if at % block == 0:
            copies[at // block].wait()
        part = held[at : at + unit].reshape(n, cols)
        moved = jnp.dot(perm, part, preferred_element_type=F32).astype(BF16)
        for j in range(pairs):
            flat[j, at : at + unit, :] = moved[j * unit : (j + 1) * unit]
        done = at + unit
        if done % block == 0:
            here = pl.ds(done - block, block)
            for slot, plane in enumerate(home_planes(place)):
                copy = pltpu.make_async_copy(
                    flat.at[plane, here], far.at[slot, here], far_sem.at[slot, done // block - 1]
                )
                copy.start()
                leaving.append(copy)
    x, core = place[0], place[1]
    rows = tiles_y * tiles_z * bulk
    out[...] = jnp.dot(
        turned[pl.ds(0, rows), :], flat[4 * (1 - x) + 2 * (1 - core)], preferred_element_type=F32
    )
    for copy in leaving:
        copy.wait()


def product_kernel(place, turned, flat, *outs, jobs, bulk, tiles_y, tiles_z):
    x, core, y = place[0], place[1], place[2]
    rows = tiles_z * bulk

    def dot(at, height, plane):
        return jnp.dot(turned[pl.ds(at, height), :], flat[plane], preferred_element_type=F32)

    for out, parts in zip(outs[:-1], jobs):
        base = 0
        for who, part in parts:
            pair = 2 * (core if who == "own" else 1 - core)
            if part == "a_away":
                out[pl.ds(base, 2 * rows), :] = dot(0, 2 * rows, 4 * (1 - x) + pair)
            elif part == "a_home":
                out[pl.ds(base, 2 * rows), :] = dot(0, 2 * rows, 4 * x + pair)
            elif part in ("b_away", "b_home"):
                side = y if part == "b_home" else 1 - y
                for xx in range(2):
                    at = pl.multiple_of(side * rows, 16)
                    out[pl.ds(base + xx * rows, rows), :] = dot(at, rows, 4 * xx + pair + 1)
            else:
                for xx in range(2):
                    for i in range(2):
                        got = dot(2 * rows, tiles_y * tiles_z * EDGE, 4 * xx + pair + i)
                        for zz in range(tiles_z):
                            for yy in range(tiles_y):
                                at = base + (((zz * 2 + xx) * tiles_y + yy) * 2 + i) * EDGE
                                out[pl.ds(at, EDGE), :] = got[(zz * tiles_y + yy) * EDGE :][:EDGE]
            base += 2 * rows if part != "c" else 4 * tiles_y * tiles_z * EDGE


def home_kernel(place, turned, far, core_a, core_b, out_a, out_b, held, sem, *, bulk, tiles_z):
    y = place[2]
    rows = tiles_z * bulk
    copies = [pltpu.make_async_copy(far.at[slot], held.at[slot], sem.at[slot]) for slot in range(3)]
    for copy in copies:
        copy.start()

    def dot(at, height, slot):
        return jnp.dot(turned[pl.ds(at, height), :], held[slot], preferred_element_type=F32)

    copies[0].wait()
    out_a[...] = core_a[...] + dot(0, 2 * rows, 0)
    for xx in range(2):
        copies[1 + xx].wait()
        here = pl.ds(xx * rows, rows)
        out_b[here, :] = core_b[here, :] + dot(pl.multiple_of(y * rows, 16), rows, 1 + xx)


def first_kernel(own, core, out):
    encode(out, own[...] + core[pl.ds(0, own.shape[0]), :])


def spread_kernel(place, own, core, keep, *outs, rows, count, base):
    z = place[3]

    def total(to):
        at = pl.multiple_of(to * rows, 16)
        return own[pl.ds(at, rows), :] + core[pl.ds(base + at, rows), :]

    for hop in range(1, count):
        encode(outs[hop - 1], total(z ^ hop))
    keep[...] = total(z)


def halve_kernel(place, own, *refs, which, rows):
    *gots, keep, out = refs
    home = place[which]

    def total(half):
        at = pl.multiple_of(half * rows, 16)
        value = own[pl.ds(at, rows), :]
        for got in gots:
            value = value + decode(got, at, rows)
        return value

    encode(out, total(1 - home))
    keep[...] = total(home)


def line_kernel(place, keep_a, got_a, keep_b, got_b, own, *outs, rows, count):
    z = place[3]

    def total(to):
        start = pl.multiple_of(to * rows, 16)
        at = pl.ds(start, rows)
        first = keep_a[at, :] + decode(got_a, start, rows)
        second = keep_b[at, :] + decode(got_b, start, rows)
        return jnp.concatenate([first, second], 0)

    for hop in range(1, count):
        encode(outs[hop - 1], total(z ^ hop))
    own[...] = total(z)


def last_kernel(own, keep_c, got_c, *refs):
    gots, (row_e, col_e, pair_e, out) = refs[:-4], refs[-4:]
    value = own[...]
    for got in gots:
        value = value + decode(got, 0, own.shape[0])
    edge = keep_c[...] + decode(got_c, 0, keep_c.shape[0])
    bulk = out.shape[1] - EDGE
    for i in range(out.shape[0]):
        denominator = row_e[...] + col_e[...] - pair_e[i]
        rows = jnp.concatenate([value[i * bulk : (i + 1) * bulk], edge[i * EDGE : (i + 1) * EDGE]], 0)
        out[i] = (rows / denominator).astype(BF16)


def swap(value, axis, bit):
    return lax.ppermute(value, axis, [(i, i ^ bit) for i in range(lax.axis_size(axis))])


def on_chip_plan(integrals, amplitudes, virt_energy, pair_energy):
    tile_size, ka_size = lax.axis_size("tile"), lax.axis_size("ka")
    tile_pos, ka_pos = lax.axis_index("tile"), lax.axis_index("ka")
    k, c, pairs, cols = amplitudes.shape
    depth, virt = k * c, integrals.shape[2]
    own_pairs, own_rows = pairs // ka_size, virt // tile_size
    tiles_y, tiles_z = 2, tile_size // 2
    hops = [hop for hop in range(2, tiles_z)] + [1]
    bulk = own_rows - EDGE
    rows = bulk * tiles_z
    edges = EDGE * tiles_y * own_pairs * 2
    place = jnp.stack([ka_pos // 2, ka_pos % 2, tile_pos % 2, tile_pos // 2]).astype(jnp.int32)
    wide = integrals.transpose(1, 0, 2).reshape(depth, virt)

    def full(height):
        return shape((height, cols), F32)

    def coded(height):
        return shape((height + PAD, cols), BF16)

    block = 160
    held = pltpu.VMEM((pairs, depth, cols), BF16)
    turned, c_a, flat, far = call(
        functools.partial(
            front_kernel, block=block, unit=32, own_rows=own_rows, tiles_y=tiles_y, tiles_z=tiles_z
        ),
        [pltpu.VMEM((virt, depth), BF16), full(2 * rows), held, pltpu.HBM((3, depth, cols), BF16)],
        place, wide, amplitudes.reshape(depth, pairs, cols), specs=[SCALAR, WHOLE, FAR], room=40, out_specs=[WHOLE] * 3 + [FAR],
        scratch=[
            pltpu.VMEM((depth, pairs, cols), BF16),
            pltpu.SemaphoreType.DMA((depth // block,)),
            pltpu.SemaphoreType.DMA((3, depth // block)),
        ],
    )

    def products(flat, *jobs, after=()):
        heights = {"a": 2 * rows, "b": 2 * rows, "c": tiles_z * edges}
        outs = [full(sum(heights[part[0]] for _, part in parts)) for parts in jobs]
        return call(
            functools.partial(product_kernel, jobs=jobs, bulk=bulk, tiles_y=tiles_y, tiles_z=tiles_z),
            outs + [held], place, turned, flat,
            specs=[SCALAR, WHOLE, WHOLE], alias={2: len(jobs)}, after=after,
        )

    g_a = swap(c_a, "ka", 1)
    c_b, c_c, flat = products(flat, [("core", "b_away")], [("core", "c")])
    g_b, g_c = swap(c_b, "ka", 1), swap(c_c, "ka", 1)
    c_ah, c_bh, flat = products(flat, [("core", "a_home")], [("core", "b_home")])
    g_ah, g_bh = swap(c_ah, "ka", 1), swap(c_bh, "ka", 1)
    o_a, o_b, o_c, flat = products(flat, *([("own", part)] for part in ("a_away", "b_away", "c")))
    (send_a,) = call(first_kernel, [coded(2 * rows)], o_a, g_a)
    got_a = swap(send_a, "ka", 2)
    (send_b,) = call(first_kernel, [coded(2 * rows)], o_b, g_b, after=[send_a])
    got_b = swap(send_b, "tile", 1)
    keep_c, *sends = call(
        functools.partial(spread_kernel, rows=edges, count=tiles_z, base=0),
        [full(edges)] + [coded(edges)] * (tiles_z - 1), place, o_c, g_c,
        specs=[SCALAR, WHOLE, WHOLE], after=[send_b],
    )
    gots_c = [swap(sends[hop - 1], "tile", 2 * hop) for hop in hops]

    h_a, h_b = call(
        functools.partial(home_kernel, bulk=bulk, tiles_z=tiles_z), [full(2 * rows), full(2 * rows)],
        place, turned, far, g_ah, g_bh, specs=[SCALAR, WHOLE, FAR, WHOLE, WHOLE], after=[keep_c], room=16,
        scratch=[pltpu.VMEM((3, depth, cols), BF16), pltpu.SemaphoreType.DMA((3,))],
    )
    mid = functools.partial(halve_kernel, rows=rows)
    specs = [SCALAR, WHOLE, WHOLE]
    keep_a, send_a = call(
        functools.partial(mid, which=2), [full(rows), coded(rows)], place, h_a, got_a, specs=specs
    )
    got_a = swap(send_a, "tile", 1)
    keep_c, send_c = call(
        functools.partial(halve_kernel, which=0, rows=edges // 2), [full(edges // 2), coded(edges // 2)],
        place, keep_c, *gots_c, specs=[SCALAR] + [WHOLE] * tiles_z, work=LONG,
    )
    got_c = swap(send_c, "ka", 2)
    keep_b, send_b = call(
        functools.partial(mid, which=0), [full(rows), coded(rows)], place, h_b, got_b,
        specs=specs, after=[keep_a],
    )
    got_b = swap(send_b, "ka", 2)

    height = own_pairs * bulk
    own, *sends = call(
        functools.partial(line_kernel, rows=bulk, count=tiles_z),
        [full(height)] + [coded(height)] * (tiles_z - 1), place, keep_a, got_a, keep_b, got_b,
        specs=[SCALAR] + [WHOLE] * 4,
    )
    gots = [swap(sends[hop - 1], "tile", 2 * hop) for hop in hops]
    keep_c, send_c = call(
        functools.partial(halve_kernel, which=2, rows=edges // 4), [full(edges // 4), coded(edges // 4)],
        place, keep_c, got_c, specs=[SCALAR, WHOLE, WHOLE], after=[own],
    )
    got_c = swap(send_c, "tile", 1)
    own_virt = lax.dynamic_slice_in_dim(virt_energy, tile_pos * own_rows, own_rows, 0)
    own_e = lax.dynamic_slice_in_dim(pair_energy, ka_pos * own_pairs, own_pairs, 0)
    (out,) = call(
        last_kernel, [shape((own_pairs, own_rows, cols), BF16)],
        own, keep_c, got_c, *gots, own_virt[:, None], virt_energy[None, :], own_e,
        specs=[WHOLE] * (3 + len(gots) + 2) + [SCALAR],
    )
    return out


def trade(parts, axis, bit, dim, wire):
    mine = (lax.axis_index(axis) // bit) % 2
    keep = lax.dynamic_index_in_dim(parts, mine, dim, keepdims=False)
    away = lax.dynamic_index_in_dim(parts, 1 - mine, dim, keepdims=False)
    got = swap(away.astype(wire), axis, bit)
    return keep + got.astype(F32)


def bits_of(size):
    return [1 << i for i in range(size.bit_length() - 1)]


def any_plan(integrals, amplitudes, virt_energy, pair_energy):
    tile_size, ka_size = lax.axis_size("tile"), lax.axis_size("ka")
    summed = jnp.einsum("cka,kcjb->jab", integrals, amplitudes, preferred_element_type=F32)
    pairs, virt, cols = summed.shape
    own_pairs, own_rows = pairs // ka_size, virt // tile_size
    ka_bits, tile_bits = bits_of(ka_size), bits_of(tile_size)
    grid = summed.reshape([2] * len(ka_bits) + [own_pairs] + [2] * len(tile_bits) + [own_rows, cols])
    for i, bit in enumerate(ka_bits):
        grid = trade(grid, "ka", bit, len(ka_bits) - 1 - i, F32)
    for i, bit in enumerate(tile_bits):
        grid = trade(grid, "tile", bit, len(tile_bits) - i, F32)
    tile_pos, ka_pos = lax.axis_index("tile"), lax.axis_index("ka")
    own_virt = lax.dynamic_slice_in_dim(virt_energy, tile_pos * own_rows, own_rows, 0)
    own_e = lax.dynamic_slice_in_dim(pair_energy, ka_pos * own_pairs, own_pairs, 0)
    denominator = own_virt[None, :, None] + virt_energy[None, None, :] - own_e[:, None, None]
    return (grid / denominator).astype(BF16)


def solution(mesh):
    fits = mesh.shape["ka"] == 4 and mesh.shape["tile"] == 8

    def per_device(integrals, amplitudes, virt_energy, pair_energy):
        own_rows = integrals.shape[2] // lax.axis_size("tile")
        depth = amplitudes.shape[0] * amplitudes.shape[1]
        plain = fits and own_rows % 16 == 0 and depth % 160 == 0 and amplitudes.shape[2] == 8
        plan = on_chip_plan if plain else any_plan
        return plan(integrals, amplitudes, virt_energy, pair_energy)

    in_specs = (P("tile", "ka", None), P("ka", "tile", None, None), P(), P())
    out_specs = P("ka", "tile", None)
    return jax.shard_map(
        per_device, mesh=mesh, in_specs=in_specs, out_specs=out_specs, check_vma=False
    )
```

```python
import functools

import jax
import jax.numpy as jnp
from jax import lax
from jax.experimental import pallas as pl
from jax.experimental.pallas import tpu as pltpu
from jax.sharding import PartitionSpec as P

F32, BF16 = jnp.float32, jnp.bfloat16
SPAN, BASE = 248.0, 124.0
EDGE = 16
LONG = 1 << 35
PAD = 8
FAR = pl.BlockSpec(memory_space=pltpu.HBM)
WHOLE = pl.BlockSpec(memory_space=pltpu.VMEM)
SCALAR = pl.BlockSpec(memory_space=pltpu.SMEM)


def shape(dims, dtype):
    return jax.ShapeDtypeStruct(tuple(dims), dtype)


def encode(out_ref, value):
    rows, cols = value.shape
    tall = value.reshape(rows // 8, 8, cols)
    size = jnp.abs(tall)
    top = jnp.maximum(jnp.max(size, axis=0) * 1.01, 1e-30).astype(BF16)
    factor = SPAN / top.astype(F32)
    code = jnp.exp2(size * factor[None] - BASE)
    code = jnp.where(tall < 0, -code, code)
    out_ref[pl.ds(0, rows), :] = code.reshape(rows, cols).astype(BF16)
    out_ref[pl.ds(rows, PAD), :] = top


def decode(ref, first, rows):
    total, cols = ref.shape[0] - PAD, ref.shape[1]
    factor = ref[pl.ds(total, PAD), :].astype(F32) * (1.0 / SPAN)
    code = ref[pl.ds(first, rows), :].astype(F32).reshape(rows // 8, 8, cols)
    size = (jnp.log2(jnp.abs(code)) + BASE) * factor[None]
    return jnp.where(code < 0, -size, size).reshape(rows, cols)


def call(kernel, outs, *args, specs=None, room=12, scratch=(), alias=None, after=(), work=1000, out_specs=None):
    specs = list(specs or [WHOLE] * len(args))
    count = len(after)

    def body(*refs):
        kernel(*refs[count:])

    return pl.pallas_call(
        body,
        in_specs=[pl.BlockSpec(memory_space=pl.ANY)] * count + specs,
        out_specs=out_specs or [WHOLE] * len(outs),
        out_shape=outs,
        scratch_shapes=scratch,
        input_output_aliases={i + count: o for i, o in (alias or {}).items()},
        compiler_params=pltpu.CompilerParams(vmem_limit_bytes=room << 20),
        cost_estimate=pl.CostEstimate(
            flops=work, bytes_accessed=1000, transcendentals=0
        ),
    )(*after, *args)


def home_planes(place):
    x, core = place[0], place[1]
    return 4 * x + 2 * core, 2 * core + 1, 4 + 2 * core + 1


def front_kernel(place, wide, amp, turned, out, flat, far, held, sem, far_sem, *, block, unit, own_rows, tiles_y, tiles_z):
    depth, pairs, cols = amp.shape
    copies = [
        pltpu.make_async_copy(amp.at[pl.ds(at, block)], held.at[pl.ds(at, block)], sem.at[at // block])
        for at in range(0, depth, block)
    ]
    for copy in copies:
        copy.start()
    t = wide[...].T
    bulk = own_rows - EDGE
    for y in range(tiles_y):
        for z in range(tiles_z):
            at = (z * tiles_y + y) * own_rows
            turned[pl.ds((y * tiles_z + z) * bulk, bulk), :] = t[at : at + bulk]
            edge = tiles_y * tiles_z * bulk + (z * tiles_y + y) * EDGE
            turned[pl.ds(edge, EDGE), :] = t[at + bulk : at + own_rows]
    leaving = []
    n = unit * pairs
    r = lax.broadcasted_iota(jnp.int32, (n, n), 0)
    c = lax.broadcasted_iota(jnp.int32, (n, n), 1)
    perm = (c == (r % unit) * pairs + r // unit).astype(F32).astype(BF16)
    for at in range(0, depth, unit):
        if at % block == 0:
            copies[at // block].wait()
        part = held[at : at + unit].reshape(n, cols)
        moved = jnp.dot(perm, part, preferred_element_type=F32).astype(BF16)
        for j in range(pairs):
            flat[j, at : at + unit, :] = moved[j * unit : (j + 1) * unit]
        done = at + unit
        if done % block == 0:
            here = pl.ds(done - block, block)
            for slot, plane in enumerate(home_planes(place)):
                copy = pltpu.make_async_copy(
                    flat.at[plane, here], far.at[slot, here], far_sem.at[slot, done // block - 1]
                )
                copy.start()
                leaving.append(copy)
    x, core = place[0], place[1]
    rows = tiles_y * tiles_z * bulk
    out[...] = jnp.dot(
        turned[pl.ds(0, rows), :], flat[4 * (1 - x) + 2 * (1 - core)], preferred_element_type=F32
    )
    for copy in leaving:
        copy.wait()


def product_kernel(place, turned, flat, *outs, jobs, bulk, tiles_y, tiles_z):
    x, core, y = place[0], place[1], place[2]
    rows = tiles_z * bulk

    def dot(at, height, plane):
        return jnp.dot(turned[pl.ds(at, height), :], flat[plane], preferred_element_type=F32)

    for out, parts in zip(outs[:-1], jobs):
        base = 0
        for who, part in parts:
            pair = 2 * (core if who == "own" else 1 - core)
            if part == "a_away":
                out[pl.ds(base, 2 * rows), :] = dot(0, 2 * rows, 4 * (1 - x) + pair)
            elif part == "a_home":
                out[pl.ds(base, 2 * rows), :] = dot(0, 2 * rows, 4 * x + pair)
            elif part in ("b_away", "b_home"):
                side = y if part == "b_home" else 1 - y
                for xx in range(2):
                    at = pl.multiple_of(side * rows, 16)
                    out[pl.ds(base + xx * rows, rows), :] = dot(at, rows, 4 * xx + pair + 1)
            else:
                for xx in range(2):
                    for i in range(2):
                        got = dot(2 * rows, tiles_y * tiles_z * EDGE, 4 * xx + pair + i)
                        for zz in range(tiles_z):
                            for yy in range(tiles_y):
                                at = base + (((zz * 2 + xx) * tiles_y + yy) * 2 + i) * EDGE
                                out[pl.ds(at, EDGE), :] = got[(zz * tiles_y + yy) * EDGE :][:EDGE]
            base += 2 * rows if part != "c" else 4 * tiles_y * tiles_z * EDGE


def home_kernel(place, turned, far, core_a, core_b, out_a, out_b, held, sem, *, bulk, tiles_z):
    y = place[2]
    rows = tiles_z * bulk
    copies = [pltpu.make_async_copy(far.at[slot], held.at[slot], sem.at[slot]) for slot in range(3)]
    for copy in copies:
        copy.start()

    def dot(at, height, slot):
        return jnp.dot(turned[pl.ds(at, height), :], held[slot], preferred_element_type=F32)

    copies[0].wait()
    out_a[...] = core_a[...] + dot(0, 2 * rows, 0)
    for xx in range(2):
        copies[1 + xx].wait()
        here = pl.ds(xx * rows, rows)
        out_b[here, :] = core_b[here, :] + dot(pl.multiple_of(y * rows, 16), rows, 1 + xx)


def first_kernel(own, core, out):
    encode(out, own[...] + core[pl.ds(0, own.shape[0]), :])


def spread_kernel(place, own, core, keep, *outs, rows, count, base):
    z = place[3]

    def total(to):
        at = pl.multiple_of(to * rows, 16)
        return own[pl.ds(at, rows), :] + core[pl.ds(base + at, rows), :]

    for hop in range(1, count):
        encode(outs[hop - 1], total(z ^ hop))
    keep[...] = total(z)


def part_of(own, gots, to, rows):
    at = pl.multiple_of(to * rows, 16)
    value = own[pl.ds(at, rows), :]
    for got in gots:
        value = value + decode(got, at, rows)
    return value


def halve_kernel(place, own, *refs, which, rows):
    *gots, keep, out = refs
    encode(out, part_of(own, gots, 1 - place[which], rows))
    keep[...] = part_of(own, gots, place[which], rows)


def away_kernel(place, own, got, out, *, which, rows):
    encode(out, part_of(own, [got], 1 - place[which], rows))


def stay_kernel(place, own_a, got_a, own_b, got_b, keep_a, keep_b, *, which_a, which_b, rows):
    keep_a[...] = part_of(own_a, [got_a], place[which_a], rows)
    keep_b[...] = part_of(own_b, [got_b], place[which_b], rows)


def line_kernel(place, keep_a, got_a, keep_b, got_b, *outs, rows, hops):
    for hop, out in zip(hops, outs):
        first = part_of(keep_a, [got_a], place[3] ^ hop, rows)
        second = part_of(keep_b, [got_b], place[3] ^ hop, rows)
        value = jnp.concatenate([first, second], 0)
        if hop:
            encode(out, value)
        else:
            out[...] = value


def rest_kernel(place, keep_a, got_a, keep_b, got_b, row_e, col_e, pair_e, own, below, *, rows):
    line_kernel(place, keep_a, got_a, keep_b, got_b, own, rows=rows, hops=[0])
    for i in range(below.shape[0]):
        below[i] = row_e[...] + col_e[...] - pair_e[i]


def bulk_kernel(own, *refs):
    gots, (below, out) = refs[:-2], refs[-2:]
    value = own[...]
    for got in gots:
        value = value + decode(got, 0, own.shape[0])
    bulk = own.shape[0] // below.shape[0]
    for i in range(below.shape[0]):
        here = pl.ds(i * bulk, bulk)
        out[here, :] = (value[i * bulk : (i + 1) * bulk] / below[i, :bulk]).astype(BF16)


def last_kernel(bulk_rows, keep_c, got_c, below, out):
    edge = keep_c[...] + decode(got_c, 0, keep_c.shape[0])
    bulk = out.shape[1] - EDGE
    for i in range(out.shape[0]):
        out[i, pl.ds(0, bulk), :] = bulk_rows[pl.ds(i * bulk, bulk), :]
        out[i, pl.ds(bulk, EDGE), :] = (edge[i * EDGE : (i + 1) * EDGE] / below[i, bulk:]).astype(BF16)


def swap(value, axis, bit):
    return lax.ppermute(value, axis, [(i, i ^ bit) for i in range(lax.axis_size(axis))])


def on_chip_plan(integrals, amplitudes, virt_energy, pair_energy):
    tile_size, ka_size = lax.axis_size("tile"), lax.axis_size("ka")
    tile_pos, ka_pos = lax.axis_index("tile"), lax.axis_index("ka")
    k, c, pairs, cols = amplitudes.shape
    depth, virt = k * c, integrals.shape[2]
    own_pairs, own_rows = pairs // ka_size, virt // tile_size
    tiles_y, tiles_z = 2, tile_size // 2
    hops = [hop for hop in range(2, tiles_z)] + [1]
    bulk = own_rows - EDGE
    rows = bulk * tiles_z
    edges = EDGE * tiles_y * own_pairs * 2
    place = jnp.stack([ka_pos // 2, ka_pos % 2, tile_pos % 2, tile_pos // 2]).astype(jnp.int32)
    wide = integrals.transpose(1, 0, 2).reshape(depth, virt)

    def full(height):
        return shape((height, cols), F32)

    def coded(height):
        return shape((height + PAD, cols), BF16)

    block = 160
    held = pltpu.VMEM((pairs, depth, cols), BF16)
    turned, c_a, flat, far = call(
        functools.partial(
            front_kernel, block=block, unit=32, own_rows=own_rows, tiles_y=tiles_y, tiles_z=tiles_z
        ),
        [pltpu.VMEM((virt, depth), BF16), full(2 * rows), held, pltpu.HBM((3, depth, cols), BF16)],
        place, wide, amplitudes.reshape(depth, pairs, cols), specs=[SCALAR, WHOLE, FAR], room=40, out_specs=[WHOLE] * 3 + [FAR],
        scratch=[
            pltpu.VMEM((depth, pairs, cols), BF16),
            pltpu.SemaphoreType.DMA((depth // block,)),
            pltpu.SemaphoreType.DMA((3, depth // block)),
        ],
    )

    def products(flat, *jobs, after=()):
        heights = {"a": 2 * rows, "b": 2 * rows, "c": tiles_z * edges}
        outs = [full(sum(heights[part[0]] for _, part in parts)) for parts in jobs]
        return call(
            functools.partial(product_kernel, jobs=jobs, bulk=bulk, tiles_y=tiles_y, tiles_z=tiles_z),
            outs + [held], place, turned, flat,
            specs=[SCALAR, WHOLE, WHOLE], alias={2: len(jobs)}, after=after,
        )

    g_a = swap(c_a, "ka", 1)
    c_b, c_c, flat = products(flat, [("core", "b_away")], [("core", "c")])
    g_b, g_c = swap(c_b, "ka", 1), swap(c_c, "ka", 1)
    c_ah, c_bh, flat = products(flat, [("core", "a_home")], [("core", "b_home")])
    g_ah, g_bh = swap(c_ah, "ka", 1), swap(c_bh, "ka", 1)
    o_a, o_b, o_c, flat = products(flat, *([("own", part)] for part in ("a_away", "b_away", "c")))
    (send_a,) = call(first_kernel, [coded(2 * rows)], o_a, g_a)
    got_a = swap(send_a, "ka", 2)
    (send_b,) = call(first_kernel, [coded(2 * rows)], o_b, g_b, after=[send_a])
    got_b = swap(send_b, "tile", 1)
    keep_c, *sends = call(
        functools.partial(spread_kernel, rows=edges, count=tiles_z, base=0),
        [full(edges)] + [coded(edges)] * (tiles_z - 1), place, o_c, g_c,
        specs=[SCALAR, WHOLE, WHOLE], after=[send_b],
    )
    gots_c = [swap(sends[hop - 1], "tile", 2 * hop) for hop in hops]

    h_a, h_b = call(
        functools.partial(home_kernel, bulk=bulk, tiles_z=tiles_z), [full(2 * rows), full(2 * rows)],
        place, turned, far, g_ah, g_bh, specs=[SCALAR, WHOLE, FAR, WHOLE, WHOLE], after=[keep_c], room=16,
        scratch=[pltpu.VMEM((3, depth, cols), BF16), pltpu.SemaphoreType.DMA((3,))],
    )
    away = functools.partial(away_kernel, rows=rows)
    specs = [SCALAR, WHOLE, WHOLE]
    (send_a,) = call(functools.partial(away, which=2), [coded(rows)], place, h_a, got_a, specs=specs)
    (send_b,) = call(
        functools.partial(away, which=0), [coded(rows)], place, h_b, got_b, specs=specs, after=[send_a]
    )
    keep_a, keep_b = call(
        functools.partial(stay_kernel, which_a=2, which_b=0, rows=rows), [full(rows)] * 2,
        place, h_a, got_a, h_b, got_b, specs=[SCALAR] + [WHOLE] * 4, after=[send_b],
    )
    got_a = swap(send_a, "tile", 1)
    got_b = swap(send_b, "ka", 2)
    keep_c, send_c = call(
        functools.partial(halve_kernel, which=0, rows=edges // 2), [full(edges // 2), coded(edges // 2)],
        place, keep_c, *gots_c, specs=[SCALAR] + [WHOLE] * tiles_z, work=LONG, after=[keep_a],
    )
    got_c = swap(send_c, "ka", 2)

    height = own_pairs * bulk
    line = functools.partial(line_kernel, rows=bulk)
    specs = [SCALAR] + [WHOLE] * 4
    sends = call(
        functools.partial(line, hops=hops), [coded(height)] * len(hops),
        place, keep_a, got_a, keep_b, got_b, specs=specs, after=[send_c],
    )
    gots = [swap(send, "tile", 2 * hop) for hop, send in zip(hops, sends)]
    keep_c, send_c = call(
        functools.partial(halve_kernel, which=2, rows=edges // 4), [full(edges // 4), coded(edges // 4)],
        place, keep_c, got_c, specs=[SCALAR, WHOLE, WHOLE], after=[sends[0]],
    )
    got_c = swap(send_c, "tile", 1)
    own_virt = lax.dynamic_slice_in_dim(virt_energy, tile_pos * own_rows, own_rows, 0)
    own_e = lax.dynamic_slice_in_dim(pair_energy, ka_pos * own_pairs, own_pairs, 0)
    own, below = call(
        functools.partial(rest_kernel, rows=bulk), [full(height), shape((own_pairs, own_rows, cols), F32)],
        place, keep_a, got_a, keep_b, got_b, own_virt[:, None], virt_energy[None, :], own_e,
        specs=specs + [WHOLE, WHOLE, SCALAR], after=[keep_c],
    )
    (bulk_rows,) = call(bulk_kernel, [shape((height, cols), BF16)], own, *gots, below)
    (out,) = call(last_kernel, [shape((own_pairs, own_rows, cols), BF16)], bulk_rows, keep_c, got_c, below)
    return out


def trade(parts, axis, bit, dim, wire):
    mine = (lax.axis_index(axis) // bit) % 2
    keep = lax.dynamic_index_in_dim(parts, mine, dim, keepdims=False)
    away = lax.dynamic_index_in_dim(parts, 1 - mine, dim, keepdims=False)
    got = swap(away.astype(wire), axis, bit)
    return keep + got.astype(F32)


def bits_of(size):
    return [1 << i for i in range(size.bit_length() - 1)]


def any_plan(integrals, amplitudes, virt_energy, pair_energy):
    tile_size, ka_size = lax.axis_size("tile"), lax.axis_size("ka")
    summed = jnp.einsum("cka,kcjb->jab", integrals, amplitudes, preferred_element_type=F32)
    pairs, virt, cols = summed.shape
    own_pairs, own_rows = pairs // ka_size, virt // tile_size
    ka_bits, tile_bits = bits_of(ka_size), bits_of(tile_size)
    grid = summed.reshape([2] * len(ka_bits) + [own_pairs] + [2] * len(tile_bits) + [own_rows, cols])
    for i, bit in enumerate(ka_bits):
        grid = trade(grid, "ka", bit, len(ka_bits) - 1 - i, F32)
    for i, bit in enumerate(tile_bits):
        grid = trade(grid, "tile", bit, len(tile_bits) - i, F32)
    tile_pos, ka_pos = lax.axis_index("tile"), lax.axis_index("ka")
    own_virt = lax.dynamic_slice_in_dim(virt_energy, tile_pos * own_rows, own_rows, 0)
    own_e = lax.dynamic_slice_in_dim(pair_energy, ka_pos * own_pairs, own_pairs, 0)
    denominator = own_virt[None, :, None] + virt_energy[None, None, :] - own_e[:, None, None]
    return (grid / denominator).astype(BF16)


def solution(mesh):
    fits = mesh.shape["ka"] == 4 and mesh.shape["tile"] == 8

    def per_device(integrals, amplitudes, virt_energy, pair_energy):
        own_rows = integrals.shape[2] // lax.axis_size("tile")
        depth = amplitudes.shape[0] * amplitudes.shape[1]
        plain = fits and own_rows % 16 == 0 and depth % 160 == 0 and amplitudes.shape[2] == 8
        plan = on_chip_plan if plain else any_plan
        return plan(integrals, amplitudes, virt_energy, pair_energy)

    in_specs = (P("tile", "ka", None), P("ka", "tile", None, None), P(), P())
    out_specs = P("ka", "tile", None)
    return jax.shard_map(
        per_device, mesh=mesh, in_specs=in_specs, out_specs=out_specs, check_vma=False
    )
```

```python
import functools

import jax
import jax.numpy as jnp
from jax import lax
from jax.experimental import pallas as pl
from jax.experimental.pallas import tpu as pltpu
from jax.sharding import PartitionSpec as P

F32, BF16 = jnp.float32, jnp.bfloat16
SPAN, BASE = 248.0, 124.0
EDGE = 16
LONG = 1 << 35
PAD = 8
FAR = pl.BlockSpec(memory_space=pltpu.HBM)
WHOLE = pl.BlockSpec(memory_space=pltpu.VMEM)
SCALAR = pl.BlockSpec(memory_space=pltpu.SMEM)


def shape(dims, dtype):
    return jax.ShapeDtypeStruct(tuple(dims), dtype)


def encode(out_ref, value):
    rows, cols = value.shape
    tall = value.reshape(rows // 8, 8, cols)
    size = jnp.abs(tall)
    top = jnp.maximum(jnp.max(size, axis=0) * 1.01, 1e-30).astype(BF16)
    factor = SPAN / top.astype(F32)
    code = jnp.exp2(size * factor[None] - BASE)
    code = jnp.where(tall < 0, -code, code)
    out_ref[pl.ds(0, rows), :] = code.reshape(rows, cols).astype(BF16)
    out_ref[pl.ds(rows, PAD), :] = top


def decode(ref, first, rows):
    total, cols = ref.shape[0] - PAD, ref.shape[1]
    factor = ref[pl.ds(total, PAD), :].astype(F32) * (1.0 / SPAN)
    code = ref[pl.ds(first, rows), :].astype(F32).reshape(rows // 8, 8, cols)
    size = (jnp.log2(jnp.abs(code)) + BASE) * factor[None]
    return jnp.where(code < 0, -size, size).reshape(rows, cols)


def call(kernel, outs, *args, specs=None, room=12, scratch=(), alias=None, after=(), work=1000, out_specs=None):
    specs = list(specs or [WHOLE] * len(args))
    count = len(after)

    def body(*refs):
        kernel(*refs[count:])

    return pl.pallas_call(
        body,
        in_specs=[pl.BlockSpec(memory_space=pl.ANY)] * count + specs,
        out_specs=out_specs or [WHOLE] * len(outs),
        out_shape=outs,
        scratch_shapes=scratch,
        input_output_aliases={i + count: o for i, o in (alias or {}).items()},
        compiler_params=pltpu.CompilerParams(vmem_limit_bytes=room << 20),
        cost_estimate=pl.CostEstimate(
            flops=work, bytes_accessed=1000, transcendentals=0
        ),
    )(*after, *args)


def plane(flat, group, side, rows=slice(None)):
    cols = flat.shape[2] // 2
    return flat.at[group, rows, pl.ds(pl.multiple_of(side * cols, 128), cols)]


def home_planes(place):
    x, core = place[0], place[1]
    return (2 * core, x), (2 * core + 1, 0), (2 * core + 1, 1)


def front_kernel(place, wide, amp, turned, out, flat, far, held, sem, far_sem, *, block, far_block, unit, own_rows, tiles_y, tiles_z):
    depth, pairs, cols = amp.shape
    virt = wide.shape[1]
    copies = [
        pltpu.make_async_copy(amp.at[pl.ds(at, block)], held.at[pl.ds(at, block)], sem.at[at // block])
        for at in range(0, depth, block)
    ]
    for copy in copies:
        copy.start()
    bulk = own_rows - EDGE

    def turn(first, count):
        t = wide[:, first : first + count].T
        for at in range(0, count, EDGE):
            tile, row = divmod(first + at, own_rows)
            z, y = divmod(tile, tiles_y)
            if row < bulk:
                to = (y * tiles_z + z) * bulk + row
            else:
                to = tiles_y * tiles_z * bulk + (z * tiles_y + y) * EDGE
            turned[to : to + EDGE, :] = t[at : at + EDGE]

    leaving = []
    n = unit * pairs
    r = lax.broadcasted_iota(jnp.int32, (n, n), 0)
    c = lax.broadcasted_iota(jnp.int32, (n, n), 1)
    perm = (c == (r % unit) * pairs + r // unit).astype(F32).astype(BF16)
    for at in range(0, depth, unit):
        if at % block == 0:
            copies[at // block].wait()
        part = held[at : at + unit].reshape(n, cols)
        moved = jnp.dot(perm, part, preferred_element_type=F32).astype(BF16)
        for j in range(pairs):
            flat[j % 4, at : at + unit, pl.ds(j // 4 * cols, cols)] = moved[j * unit : (j + 1) * unit]
        if at // unit % 4 == 2 and at // unit // 4 < virt // 128:
            turn(at // unit // 4 * 128, 128)
        done = at + unit
        if done % far_block == 0:
            here = pl.ds(done - far_block, far_block)
            for slot, (group, side) in enumerate(home_planes(place)):
                copy = pltpu.make_async_copy(
                    plane(flat, group, side, here), far.at[slot, here], far_sem.at[slot, done // far_block - 1]
                )
                copy.start()
                leaving.append(copy)
    x, core = place[0], place[1]
    rows = tiles_y * tiles_z * bulk
    out[...] = jnp.dot(
        turned[pl.ds(0, rows), :], plane(flat, 2 * (1 - core), 1 - x)[...], preferred_element_type=F32
    )
    for copy in leaving:
        copy.wait()


def product_kernel(place, turned, flat, *outs, jobs, bulk, tiles_y, tiles_z):
    x, core, y = place[0], place[1], place[2]
    rows = tiles_z * bulk

    cols = flat.shape[2] // 2

    def dot(at, height, group, side=None):
        rhs = flat.at[group] if side is None else plane(flat, group, side)
        return jnp.dot(turned[pl.ds(at, height), :], rhs[...], preferred_element_type=F32)

    for out, parts in zip(outs[:-1], jobs):
        base = 0
        for who, part in parts:
            pair = 2 * (core if who == "own" else 1 - core)
            if part == "a_away":
                out[pl.ds(base, 2 * rows), :] = dot(0, 2 * rows, pair, 1 - x)
            elif part == "a_home":
                out[pl.ds(base, 2 * rows), :] = dot(0, 2 * rows, pair, x)
            elif part in ("b_away", "b_home"):
                side = y if part == "b_home" else 1 - y
                got = dot(pl.multiple_of(side * rows, 16), rows, pair + 1)
                for xx in range(2):
                    out[pl.ds(base + xx * rows, rows), :] = got[:, xx * cols :][:, :cols]
            else:
                for i in range(2):
                    wide = dot(2 * rows, tiles_y * tiles_z * EDGE, pair + i)
                    for xx in range(2):
                        got = wide[:, xx * cols :][:, :cols]
                        for zz in range(tiles_z):
                            for yy in range(tiles_y):
                                at = base + (((zz * tiles_y + yy) * 2 + xx) * 2 + i) * EDGE
                                out[pl.ds(at, EDGE), :] = got[(zz * tiles_y + yy) * EDGE :][:EDGE]
            base += 2 * rows if part != "c" else 4 * tiles_y * tiles_z * EDGE


def home_kernel(place, turned, far, core_a, core_b, out_a, out_b, held, sem, *, bulk, tiles_z):
    y = place[2]
    rows = tiles_z * bulk
    copies = [pltpu.make_async_copy(far.at[slot], held.at[slot], sem.at[slot]) for slot in range(3)]
    for copy in copies:
        copy.start()

    def dot(at, height, slot):
        return jnp.dot(turned[pl.ds(at, height), :], held[slot], preferred_element_type=F32)

    copies[0].wait()
    out_a[...] = core_a[...] + dot(0, 2 * rows, 0)
    for xx in range(2):
        copies[1 + xx].wait()
        here = pl.ds(xx * rows, rows)
        out_b[here, :] = core_b[here, :] + dot(pl.multiple_of(y * rows, 16), rows, 1 + xx)


def first_kernel(own, core, out):
    encode(out, own[...] + core[pl.ds(0, own.shape[0]), :])


def spread_kernel(place, own, core, keep, *outs, rows, count, base):
    z = place[3]

    def total(to):
        at = pl.multiple_of(to * rows, 16)
        return own[pl.ds(at, rows), :] + core[pl.ds(base + at, rows), :]

    for hop in range(1, count):
        encode(outs[hop - 1], total(z ^ hop))
    keep[...] = total(z)


def part_of(own, gots, to, rows):
    at = pl.multiple_of(to * rows, 16)
    value = own[pl.ds(at, rows), :]
    for got in gots:
        value = value + decode(got, at, rows)
    return value


def halve_kernel(place, own, *refs, which, rows):
    *gots, keep, out = refs
    encode(out, part_of(own, gots, 1 - place[which], rows))
    keep[...] = part_of(own, gots, place[which], rows)


def away_kernel(place, own, got, out, *, which, rows):
    encode(out, part_of(own, [got], 1 - place[which], rows))


def stay_kernel(place, own_a, got_a, own_b, got_b, keep_a, keep_b, *, which_a, which_b, rows):
    keep_a[...] = part_of(own_a, [got_a], place[which_a], rows)
    keep_b[...] = part_of(own_b, [got_b], place[which_b], rows)


def line_kernel(place, keep_a, got_a, keep_b, got_b, *outs, rows, hops):
    for hop, out in zip(hops, outs):
        first = part_of(keep_a, [got_a], place[3] ^ hop, rows)
        second = part_of(keep_b, [got_b], place[3] ^ hop, rows)
        value = jnp.concatenate([first, second], 0)
        if hop:
            encode(out, value)
        else:
            out[...] = value


def rest_kernel(place, keep_a, got_a, keep_b, got_b, row_e, col_e, pair_e, own, below, *, rows):
    line_kernel(place, keep_a, got_a, keep_b, got_b, own, rows=rows, hops=[0])
    for i in range(below.shape[0]):
        below[i] = row_e[...] + col_e[...] - pair_e[i]


def bulk_kernel(own, *refs):
    gots, (below, out) = refs[:-2], refs[-2:]
    value = own[...]
    for got in gots:
        value = value + decode(got, 0, own.shape[0])
    bulk = own.shape[0] // below.shape[0]
    for i in range(below.shape[0]):
        here = pl.ds(i * bulk, bulk)
        out[here, :] = (value[i * bulk : (i + 1) * bulk] / below[i, :bulk]).astype(BF16)


def last_kernel(bulk_rows, keep_c, got_c, below, out):
    edge = keep_c[...] + decode(got_c, 0, keep_c.shape[0])
    bulk = out.shape[1] - EDGE
    for i in range(out.shape[0]):
        out[i, pl.ds(0, bulk), :] = bulk_rows[pl.ds(i * bulk, bulk), :]
        out[i, pl.ds(bulk, EDGE), :] = (edge[i * EDGE : (i + 1) * EDGE] / below[i, bulk:]).astype(BF16)


def swap(value, axis, bit):
    return lax.ppermute(value, axis, [(i, i ^ bit) for i in range(lax.axis_size(axis))])


def on_chip_plan(integrals, amplitudes, virt_energy, pair_energy):
    tile_size, ka_size = lax.axis_size("tile"), lax.axis_size("ka")
    tile_pos, ka_pos = lax.axis_index("tile"), lax.axis_index("ka")
    k, c, pairs, cols = amplitudes.shape
    depth, virt = k * c, integrals.shape[2]
    own_pairs, own_rows = pairs // ka_size, virt // tile_size
    tiles_y, tiles_z = 2, tile_size // 2
    hops = [hop for hop in range(2, tiles_z)] + [1]
    bulk = own_rows - EDGE
    rows = bulk * tiles_z
    edges = EDGE * tiles_y * own_pairs * 2
    place = jnp.stack([ka_pos // 2, ka_pos % 2, tile_pos % 2, tile_pos // 2]).astype(jnp.int32)
    wide = integrals.transpose(1, 0, 2).reshape(depth, virt)

    def full(height):
        return shape((height, cols), F32)

    def coded(height):
        return shape((height + PAD, cols), BF16)

    block, far_block = 320, 320
    held = pltpu.VMEM((pairs // 2, depth, 2 * cols), BF16)
    turned, c_a, flat, far = call(
        functools.partial(
            front_kernel, block=block, far_block=far_block, unit=32, own_rows=own_rows, tiles_y=tiles_y, tiles_z=tiles_z
        ),
        [pltpu.VMEM((virt, depth), BF16), full(2 * rows), held, pltpu.HBM((3, depth, cols), BF16)],
        place, wide, amplitudes.reshape(depth, pairs, cols), specs=[SCALAR, WHOLE, FAR], room=40, out_specs=[WHOLE] * 3 + [FAR],
        scratch=[
            pltpu.VMEM((depth, pairs, cols), BF16),
            pltpu.SemaphoreType.DMA((depth // block,)),
            pltpu.SemaphoreType.DMA((3, depth // far_block)),
        ],
    )

    def products(flat, *jobs, after=()):
        heights = {"a": 2 * rows, "b": 2 * rows, "c": tiles_z * edges}
        outs = [full(sum(heights[part[0]] for _, part in parts)) for parts in jobs]
        return call(
            functools.partial(product_kernel, jobs=jobs, bulk=bulk, tiles_y=tiles_y, tiles_z=tiles_z),
            outs + [held], place, turned, flat,
            specs=[SCALAR, WHOLE, WHOLE], alias={2: len(jobs)}, after=after,
        )

    g_a = swap(c_a, "ka", 1)
    c_b, c_c, flat = products(flat, [("core", "b_away")], [("core", "c")])
    g_b, g_c = swap(c_b, "ka", 1), swap(c_c, "ka", 1)
    c_ah, c_bh, flat = products(flat, [("core", "a_home")], [("core", "b_home")])
    g_ah, g_bh = swap(c_ah, "ka", 1), swap(c_bh, "ka", 1)
    o_a, o_b, o_c, flat = products(flat, *([("own", part)] for part in ("a_away", "b_away", "c")))
    (send_a,) = call(first_kernel, [coded(2 * rows)], o_a, g_a)
    got_a = swap(send_a, "ka", 2)
    (send_b,) = call(first_kernel, [coded(2 * rows)], o_b, g_b, after=[send_a])
    got_b = swap(send_b, "tile", 1)
    keep_c, *sends = call(
        functools.partial(spread_kernel, rows=edges, count=tiles_z, base=0),
        [full(edges)] + [coded(edges)] * (tiles_z - 1), place, o_c, g_c,
        specs=[SCALAR, WHOLE, WHOLE], after=[send_b],
    )
    gots_c = [swap(sends[hop - 1], "tile", 2 * hop) for hop in hops]

    h_a, h_b = call(
        functools.partial(home_kernel, bulk=bulk, tiles_z=tiles_z), [full(2 * rows), full(2 * rows)],
        place, turned, far, g_ah, g_bh, specs=[SCALAR, WHOLE, FAR, WHOLE, WHOLE], after=[keep_c], room=16,
        scratch=[pltpu.VMEM((3, depth, cols), BF16), pltpu.SemaphoreType.DMA((3,))],
    )
    away = functools.partial(away_kernel, rows=rows)
    specs = [SCALAR, WHOLE, WHOLE]
    (send_a,) = call(functools.partial(away, which=2), [coded(rows)], place, h_a, got_a, specs=specs)
    (send_b,) = call(
        functools.partial(away, which=0), [coded(rows)], place, h_b, got_b, specs=specs, after=[send_a]
    )
    keep_a, keep_b = call(
        functools.partial(stay_kernel, which_a=2, which_b=0, rows=rows), [full(rows)] * 2,
        place, h_a, got_a, h_b, got_b, specs=[SCALAR] + [WHOLE] * 4, after=[send_b],
    )
    got_a = swap(send_a, "tile", 1)
    got_b = swap(send_b, "ka", 2)
    keep_c, send_c = call(
        functools.partial(halve_kernel, which=2, rows=edges // 2), [full(edges // 2), coded(edges // 2)],
        place, keep_c, *gots_c, specs=[SCALAR] + [WHOLE] * tiles_z, work=LONG, after=[keep_a],
    )
    got_c = swap(send_c, "tile", 1)

    height = own_pairs * bulk
    line = functools.partial(line_kernel, rows=bulk)
    specs = [SCALAR] + [WHOLE] * 4
    sends = call(
        functools.partial(line, hops=hops), [coded(height)] * len(hops),
        place, keep_a, got_a, keep_b, got_b, specs=specs, after=[send_c],
    )
    gots = [swap(send, "tile", 2 * hop) for hop, send in zip(hops, sends)]
    keep_c, send_c = call(
        functools.partial(halve_kernel, which=0, rows=edges // 4), [full(edges // 4), coded(edges // 4)],
        place, keep_c, got_c, specs=[SCALAR, WHOLE, WHOLE], after=[sends[0]],
    )
    got_c = swap(send_c, "ka", 2)
    own_virt = lax.dynamic_slice_in_dim(virt_energy, tile_pos * own_rows, own_rows, 0)
    own_e = lax.dynamic_slice_in_dim(pair_energy, ka_pos * own_pairs, own_pairs, 0)
    own, below = call(
        functools.partial(rest_kernel, rows=bulk), [full(height), shape((own_pairs, own_rows, cols), F32)],
        place, keep_a, got_a, keep_b, got_b, own_virt[:, None], virt_energy[None, :], own_e,
        specs=specs + [WHOLE, WHOLE, SCALAR], after=[keep_c],
    )
    (bulk_rows,) = call(bulk_kernel, [shape((height, cols), BF16)], own, *gots, below)
    (out,) = call(last_kernel, [shape((own_pairs, own_rows, cols), BF16)], bulk_rows, keep_c, got_c, below)
    return out


def trade(parts, axis, bit, dim, wire):
    mine = (lax.axis_index(axis) // bit) % 2
    keep = lax.dynamic_index_in_dim(parts, mine, dim, keepdims=False)
    away = lax.dynamic_index_in_dim(parts, 1 - mine, dim, keepdims=False)
    got = swap(away.astype(wire), axis, bit)
    return keep + got.astype(F32)


def bits_of(size):
    return [1 << i for i in range(size.bit_length() - 1)]


def any_plan(integrals, amplitudes, virt_energy, pair_energy):
    tile_size, ka_size = lax.axis_size("tile"), lax.axis_size("ka")
    summed = jnp.einsum("cka,kcjb->jab", integrals, amplitudes, preferred_element_type=F32)
    pairs, virt, cols = summed.shape
    own_pairs, own_rows = pairs // ka_size, virt // tile_size
    ka_bits, tile_bits = bits_of(ka_size), bits_of(tile_size)
    grid = summed.reshape([2] * len(ka_bits) + [own_pairs] + [2] * len(tile_bits) + [own_rows, cols])
    for i, bit in enumerate(ka_bits):
        grid = trade(grid, "ka", bit, len(ka_bits) - 1 - i, F32)
    for i, bit in enumerate(tile_bits):
        grid = trade(grid, "tile", bit, len(tile_bits) - i, F32)
    tile_pos, ka_pos = lax.axis_index("tile"), lax.axis_index("ka")
    own_virt = lax.dynamic_slice_in_dim(virt_energy, tile_pos * own_rows, own_rows, 0)
    own_e = lax.dynamic_slice_in_dim(pair_energy, ka_pos * own_pairs, own_pairs, 0)
    denominator = own_virt[None, :, None] + virt_energy[None, None, :] - own_e[:, None, None]
    return (grid / denominator).astype(BF16)


def solution(mesh):
    fits = mesh.shape["ka"] == 4 and mesh.shape["tile"] == 8

    def per_device(integrals, amplitudes, virt_energy, pair_energy):
        own_rows = integrals.shape[2] // lax.axis_size("tile")
        depth = amplitudes.shape[0] * amplitudes.shape[1]
        plain = fits and own_rows % 16 == 0 and depth % 960 == 0 and amplitudes.shape[2] == 8
        plain = plain and integrals.shape[2] % 128 == 0 and depth // 128 >= integrals.shape[2] // 128
        plan = on_chip_plan if plain else any_plan
        return plan(integrals, amplitudes, virt_energy, pair_energy)

    in_specs = (P("tile", "ka", None), P("ka", "tile", None, None), P(), P())
    out_specs = P("ka", "tile", None)
    return jax.shard_map(
        per_device, mesh=mesh, in_specs=in_specs, out_specs=out_specs, check_vma=False
    )
```

```python
import functools

import jax
import jax.numpy as jnp
from jax import lax
from jax.experimental import pallas as pl
from jax.experimental.pallas import tpu as pltpu
from jax.sharding import PartitionSpec as P

F32, BF16 = jnp.float32, jnp.bfloat16
SPAN, BASE = 248.0, 124.0
EDGE = 16
LONG = 1 << 35
PAD = 8
FAR = pl.BlockSpec(memory_space=pltpu.HBM)
WHOLE = pl.BlockSpec(memory_space=pltpu.VMEM)
SCALAR = pl.BlockSpec(memory_space=pltpu.SMEM)


def shape(dims, dtype):
    return jax.ShapeDtypeStruct(tuple(dims), dtype)


def encode(out_ref, value):
    rows, cols = value.shape
    tall = value.reshape(rows // 8, 8, cols)
    size = jnp.abs(tall)
    top = jnp.maximum(jnp.max(size, axis=0) * 1.01, 1e-30).astype(BF16)
    factor = SPAN / top.astype(F32)
    code = jnp.exp2(size * factor[None] - BASE)
    code = jnp.where(tall < 0, -code, code)
    out_ref[pl.ds(0, rows), :] = code.reshape(rows, cols).astype(BF16)
    out_ref[pl.ds(rows, PAD), :] = top


def decode(ref, first, rows):
    total, cols = ref.shape[0] - PAD, ref.shape[1]
    factor = ref[pl.ds(total, PAD), :].astype(F32) * (1.0 / SPAN)
    code = ref[pl.ds(first, rows), :].astype(F32).reshape(rows // 8, 8, cols)
    size = (jnp.log2(jnp.abs(code)) + BASE) * factor[None]
    return jnp.where(code < 0, -size, size).reshape(rows, cols)


def call(kernel, outs, *args, specs=None, room=12, scratch=(), alias=None, after=(), work=1000, out_specs=None):
    specs = list(specs or [WHOLE] * len(args))
    count = len(after)

    def body(*refs):
        kernel(*refs[count:])

    return pl.pallas_call(
        body,
        in_specs=[pl.BlockSpec(memory_space=pl.ANY)] * count + specs,
        out_specs=out_specs or [WHOLE] * len(outs),
        out_shape=outs,
        scratch_shapes=scratch,
        input_output_aliases={i + count: o for i, o in (alias or {}).items()},
        compiler_params=pltpu.CompilerParams(vmem_limit_bytes=room << 20),
        cost_estimate=pl.CostEstimate(
            flops=work, bytes_accessed=1000, transcendentals=0
        ),
    )(*after, *args)


def plane(flat, group, side, rows=slice(None)):
    cols = flat.shape[2] // 2
    return flat.at[group, rows, pl.ds(pl.multiple_of(side * cols, 128), cols)]


def home_planes(place):
    x, core = place[0], place[1]
    return (2 * core, x), (2 * core + 1, 0), (2 * core + 1, 1), (2 * core, 1 - x)


def front_kernel(place, wide, amp, turned, out, flat, far, held, sem, far_sem, *, block, far_block, unit, own_rows, tiles_y, tiles_z):
    depth, pairs, cols = amp.shape
    virt = wide.shape[1]
    copies = [
        pltpu.make_async_copy(amp.at[pl.ds(at, block)], held.at[pl.ds(at, block)], sem.at[at // block])
        for at in range(0, depth, block)
    ]
    for copy in copies:
        copy.start()
    bulk = own_rows - EDGE

    def turn(first, count):
        t = wide[:, first : first + count].T
        for at in range(0, count, EDGE):
            tile, row = divmod(first + at, own_rows)
            z, y = divmod(tile, tiles_y)
            if row < bulk:
                to = (y * tiles_z + z) * bulk + row
            else:
                to = tiles_y * tiles_z * bulk + (z * tiles_y + y) * EDGE
            turned[to : to + EDGE, :] = t[at : at + EDGE]

    leaving = []
    n = unit * pairs
    r = lax.broadcasted_iota(jnp.int32, (n, n), 0)
    c = lax.broadcasted_iota(jnp.int32, (n, n), 1)
    perm = (c == (r % unit) * pairs + r // unit).astype(F32).astype(BF16)
    for at in range(0, depth, unit):
        if at % block == 0:
            copies[at // block].wait()
        part = held[at : at + unit].reshape(n, cols)
        moved = jnp.dot(perm, part, preferred_element_type=F32).astype(BF16)
        for j in range(pairs):
            flat[j % 4, at : at + unit, pl.ds(j // 4 * cols, cols)] = moved[j * unit : (j + 1) * unit]
        if at // unit % 4 == 2 and at // unit // 4 < virt // 128:
            turn(at // unit // 4 * 128, 128)
        done = at + unit
        if done % far_block == 0:
            here = pl.ds(done - far_block, far_block)
            for slot, (group, side) in enumerate(home_planes(place)):
                copy = pltpu.make_async_copy(
                    plane(flat, group, side, here), far.at[slot, here], far_sem.at[slot, done // far_block - 1]
                )
                copy.start()
                leaving.append(copy)
    x, core = place[0], place[1]
    rows = tiles_y * tiles_z * bulk
    out[...] = jnp.dot(
        turned[pl.ds(0, rows), :], plane(flat, 2 * (1 - core), 1 - x)[...], preferred_element_type=F32
    )
    for copy in leaving:
        copy.wait()


def product_kernel(place, turned, flat, *outs, jobs, bulk, tiles_y, tiles_z):
    x, core, y = place[0], place[1], place[2]
    rows = tiles_z * bulk

    cols = flat.shape[2] // 2

    def dot(at, height, group, side=None):
        rhs = flat.at[group] if side is None else plane(flat, group, side)
        return jnp.dot(turned[pl.ds(at, height), :], rhs[...], preferred_element_type=F32)

    for out, parts in zip(outs[:-1], jobs):
        base = 0
        for who, part in parts:
            pair = 2 * (core if who == "own" else 1 - core)
            if part == "a_away":
                out[pl.ds(base, 2 * rows), :] = dot(0, 2 * rows, pair, 1 - x)
            elif part == "a_home":
                out[pl.ds(base, 2 * rows), :] = dot(0, 2 * rows, pair, x)
            elif part in ("b_away", "b_home"):
                side = y if part == "b_home" else 1 - y
                got = dot(pl.multiple_of(side * rows, 16), rows, pair + 1)
                for xx in range(2):
                    out[pl.ds(base + xx * rows, rows), :] = got[:, xx * cols :][:, :cols]
            else:
                for i in range(2):
                    wide = dot(2 * rows, tiles_y * tiles_z * EDGE, pair + i)
                    for xx in range(2):
                        got = wide[:, xx * cols :][:, :cols]
                        for zz in range(tiles_z):
                            for yy in range(tiles_y):
                                at = base + (((zz * tiles_y + yy) * 2 + xx) * 2 + i) * EDGE
                                out[pl.ds(at, EDGE), :] = got[(zz * tiles_y + yy) * EDGE :][:EDGE]
            base += 2 * rows if part != "c" else 4 * tiles_y * tiles_z * EDGE


def home_kernel(place, turned, far, core_a, core_b, out_a, out_b, held, sem, *, bulk, tiles_z):
    y = place[2]
    rows = tiles_z * bulk
    copies = [pltpu.make_async_copy(far.at[slot], held.at[slot], sem.at[slot]) for slot in range(3)]
    for copy in copies:
        copy.start()

    def dot(at, height, slot):
        return jnp.dot(turned[pl.ds(at, height), :], held[slot], preferred_element_type=F32)

    copies[0].wait()
    out_a[...] = core_a[...] + dot(0, 2 * rows, 0)
    for xx in range(2):
        copies[1 + xx].wait()
        here = pl.ds(xx * rows, rows)
        out_b[here, :] = core_b[here, :] + dot(pl.multiple_of(y * rows, 16), rows, 1 + xx)


def edge_kernel(place, turned, far, out, held, sem, *, first, tiles_y, tiles_z):
    x = place[0]
    copies = [pltpu.make_async_copy(far.at[slot], held.at[slot], sem.at[slot]) for slot in range(4)]
    for copy in copies:
        copy.start()
    for slot, (xx, i) in enumerate(((x, 0), (0, 1), (1, 1), (1 - x, 0))):
        copies[slot].wait()
        got = jnp.dot(
            turned[pl.ds(first, tiles_y * tiles_z * EDGE), :], held[slot], preferred_element_type=F32
        )
        for z in range(tiles_z):
            for y in range(tiles_y):
                at = pl.multiple_of((((z * tiles_y + y) * 2 + xx) * 2 + i) * EDGE, EDGE)
                out[pl.ds(at, EDGE), :] = got[(z * tiles_y + y) * EDGE :][:EDGE]


def first_kernel(own, core, out):
    encode(out, own[...] + core[pl.ds(0, own.shape[0]), :])


def spread_kernel(place, own, core, keep, *outs, rows, count, base):
    z = place[3]

    def total(to):
        at = pl.multiple_of(to * rows, 16)
        return own[pl.ds(at, rows), :] + core[pl.ds(base + at, rows), :]

    for hop in range(1, count):
        encode(outs[hop - 1], total(z ^ hop))
    keep[...] = total(z)


def part_of(own, gots, to, rows):
    at = pl.multiple_of(to * rows, 16)
    value = own[pl.ds(at, rows), :]
    for got in gots:
        value = value + decode(got, at, rows)
    return value


def halve_kernel(place, own, *refs, which, rows):
    *gots, keep, out = refs
    encode(out, part_of(own, gots, 1 - place[which], rows))
    keep[...] = part_of(own, gots, place[which], rows)


def away_kernel(place, own, got, out, *, which, rows):
    encode(out, part_of(own, [got], 1 - place[which], rows))


def stay_kernel(place, own_a, got_a, own_b, got_b, keep_a, keep_b, *, which_a, which_b, rows):
    keep_a[...] = part_of(own_a, [got_a], place[which_a], rows)
    keep_b[...] = part_of(own_b, [got_b], place[which_b], rows)


def line_kernel(place, keep_a, got_a, keep_b, got_b, *outs, rows, hops):
    for hop, out in zip(hops, outs):
        first = part_of(keep_a, [got_a], place[3] ^ hop, rows)
        second = part_of(keep_b, [got_b], place[3] ^ hop, rows)
        value = jnp.concatenate([first, second], 0)
        if hop:
            encode(out, value)
        else:
            out[...] = value


def rest_kernel(place, keep_a, got_a, keep_b, got_b, row_e, col_e, pair_e, own, below, *, rows):
    line_kernel(place, keep_a, got_a, keep_b, got_b, own, rows=rows, hops=[0])
    for i in range(below.shape[0]):
        below[i] = row_e[...] + col_e[...] - pair_e[i]


def bulk_kernel(own, *refs):
    gots, (below, out) = refs[:-2], refs[-2:]
    value = own[...]
    for got in gots:
        value = value + decode(got, 0, own.shape[0])
    bulk = own.shape[0] // below.shape[0]
    for i in range(below.shape[0]):
        here = pl.ds(i * bulk, bulk)
        out[here, :] = (value[i * bulk : (i + 1) * bulk] / below[i, :bulk]).astype(BF16)


def last_kernel(bulk_rows, keep_c, got_c, below, out):
    edge = keep_c[...] + decode(got_c, 0, keep_c.shape[0])
    bulk = out.shape[1] - EDGE
    for i in range(out.shape[0]):
        out[i, pl.ds(0, bulk), :] = bulk_rows[pl.ds(i * bulk, bulk), :]
        out[i, pl.ds(bulk, EDGE), :] = (edge[i * EDGE : (i + 1) * EDGE] / below[i, bulk:]).astype(BF16)


def swap(value, axis, bit):
    return lax.ppermute(value, axis, [(i, i ^ bit) for i in range(lax.axis_size(axis))])


def on_chip_plan(integrals, amplitudes, virt_energy, pair_energy):
    tile_size, ka_size = lax.axis_size("tile"), lax.axis_size("ka")
    tile_pos, ka_pos = lax.axis_index("tile"), lax.axis_index("ka")
    k, c, pairs, cols = amplitudes.shape
    depth, virt = k * c, integrals.shape[2]
    own_pairs, own_rows = pairs // ka_size, virt // tile_size
    tiles_y, tiles_z = 2, tile_size // 2
    hops = [2, 1] + [hop for hop in range(3, tiles_z)]
    bulk = own_rows - EDGE
    rows = bulk * tiles_z
    edges = EDGE * tiles_y * own_pairs * 2
    place = jnp.stack([ka_pos // 2, ka_pos % 2, tile_pos % 2, tile_pos // 2]).astype(jnp.int32)
    wide = integrals.transpose(1, 0, 2).reshape(depth, virt)

    def full(height):
        return shape((height, cols), F32)

    def coded(height):
        return shape((height + PAD, cols), BF16)

    block, far_block = 320, 320
    held = pltpu.VMEM((pairs // 2, depth, 2 * cols), BF16)
    turned, c_a, flat, far = call(
        functools.partial(
            front_kernel, block=block, far_block=far_block, unit=32, own_rows=own_rows, tiles_y=tiles_y, tiles_z=tiles_z
        ),
        [pltpu.VMEM((virt, depth), BF16), full(2 * rows), held, pltpu.HBM((4, depth, cols), BF16)],
        place, wide, amplitudes.reshape(depth, pairs, cols), specs=[SCALAR, WHOLE, FAR], room=40, out_specs=[WHOLE] * 3 + [FAR],
        scratch=[
            pltpu.VMEM((depth, pairs, cols), BF16),
            pltpu.SemaphoreType.DMA((depth // block,)),
            pltpu.SemaphoreType.DMA((4, depth // far_block)),
        ],
    )

    def products(flat, *jobs, after=()):
        heights = {"a": 2 * rows, "b": 2 * rows, "c": tiles_z * edges}
        outs = [full(sum(heights[part[0]] for _, part in parts)) for parts in jobs]
        return call(
            functools.partial(product_kernel, jobs=jobs, bulk=bulk, tiles_y=tiles_y, tiles_z=tiles_z),
            outs + [held], place, turned, flat,
            specs=[SCALAR, WHOLE, WHOLE], alias={2: len(jobs)}, after=after,
        )

    g_a = swap(c_a, "ka", 1)
    c_b, c_c, flat = products(flat, [("core", "b_away")], [("core", "c")])
    g_b, g_c = swap(c_b, "ka", 1), swap(c_c, "ka", 1)
    c_ah, c_bh, flat = products(flat, [("core", "a_home")], [("core", "b_home")])
    g_ah, g_bh = swap(c_ah, "ka", 1), swap(c_bh, "ka", 1)
    o_a, o_b, flat = products(flat, *([("own", part)] for part in ("a_away", "b_away")))
    (send_a,) = call(first_kernel, [coded(2 * rows)], o_a, g_a)
    got_a = swap(send_a, "ka", 2)
    (send_b,) = call(first_kernel, [coded(2 * rows)], o_b, g_b, after=[send_a])
    got_b = swap(send_b, "tile", 1)
    (o_c,) = call(
        functools.partial(edge_kernel, first=2 * rows, tiles_y=tiles_y, tiles_z=tiles_z),
        [full(tiles_z * edges)], place, turned, far, specs=[SCALAR, WHOLE, FAR], after=[send_b], room=16,
        scratch=[pltpu.VMEM((4, depth, cols), BF16), pltpu.SemaphoreType.DMA((4,))],
    )
    keep_c, *sends = call(
        functools.partial(spread_kernel, rows=edges, count=tiles_z, base=0),
        [full(edges)] + [coded(edges)] * (tiles_z - 1), place, o_c, g_c,
        specs=[SCALAR, WHOLE, WHOLE], after=[send_b],
    )
    gots_c = [swap(sends[hop - 1], "tile", 2 * hop) for hop in hops]

    h_a, h_b = call(
        functools.partial(home_kernel, bulk=bulk, tiles_z=tiles_z), [full(2 * rows), full(2 * rows)],
        place, turned, far, g_ah, g_bh, specs=[SCALAR, WHOLE, FAR, WHOLE, WHOLE], after=[keep_c], room=16,
        scratch=[pltpu.VMEM((3, depth, cols), BF16), pltpu.SemaphoreType.DMA((3,))],
    )
    away = functools.partial(away_kernel, rows=rows)
    specs = [SCALAR, WHOLE, WHOLE]
    (send_a,) = call(functools.partial(away, which=2), [coded(rows)], place, h_a, got_a, specs=specs)
    (send_b,) = call(
        functools.partial(away, which=0), [coded(rows)], place, h_b, got_b, specs=specs, after=[send_a]
    )
    keep_a, keep_b = call(
        functools.partial(stay_kernel, which_a=2, which_b=0, rows=rows), [full(rows)] * 2,
        place, h_a, got_a, h_b, got_b, specs=[SCALAR] + [WHOLE] * 4, after=[send_b],
    )
    got_a = swap(send_a, "tile", 1)
    got_b = swap(send_b, "ka", 2)
    keep_c, send_c = call(
        functools.partial(halve_kernel, which=2, rows=edges // 2), [full(edges // 2), coded(edges // 2)],
        place, keep_c, *gots_c, specs=[SCALAR] + [WHOLE] * tiles_z, work=LONG, after=[keep_a],
    )
    got_c = swap(send_c, "tile", 1)

    height = own_pairs * bulk
    line = functools.partial(line_kernel, rows=bulk)
    specs = [SCALAR] + [WHOLE] * 4
    sends = call(
        functools.partial(line, hops=hops), [coded(height)] * len(hops),
        place, keep_a, got_a, keep_b, got_b, specs=specs, after=[send_c],
    )
    gots = [swap(send, "tile", 2 * hop) for hop, send in zip(hops, sends)]
    keep_c, send_c = call(
        functools.partial(halve_kernel, which=0, rows=edges // 4), [full(edges // 4), coded(edges // 4)],
        place, keep_c, got_c, specs=[SCALAR, WHOLE, WHOLE], after=[sends[0]],
    )
    got_c = swap(send_c, "ka", 2)
    own_virt = lax.dynamic_slice_in_dim(virt_energy, tile_pos * own_rows, own_rows, 0)
    own_e = lax.dynamic_slice_in_dim(pair_energy, ka_pos * own_pairs, own_pairs, 0)
    own, below = call(
        functools.partial(rest_kernel, rows=bulk), [full(height), shape((own_pairs, own_rows, cols), F32)],
        place, keep_a, got_a, keep_b, got_b, own_virt[:, None], virt_energy[None, :], own_e,
        specs=specs + [WHOLE, WHOLE, SCALAR], after=[keep_c],
    )
    (bulk_rows,) = call(bulk_kernel, [shape((height, cols), BF16)], own, *gots, below)
    (out,) = call(last_kernel, [shape((own_pairs, own_rows, cols), BF16)], bulk_rows, keep_c, got_c, below)
    return out


def trade(parts, axis, bit, dim, wire):
    mine = (lax.axis_index(axis) // bit) % 2
    keep = lax.dynamic_index_in_dim(parts, mine, dim, keepdims=False)
    away = lax.dynamic_index_in_dim(parts, 1 - mine, dim, keepdims=False)
    got = swap(away.astype(wire), axis, bit)
    return keep + got.astype(F32)


def bits_of(size):
    return [1 << i for i in range(size.bit_length() - 1)]


def any_plan(integrals, amplitudes, virt_energy, pair_energy):
    tile_size, ka_size = lax.axis_size("tile"), lax.axis_size("ka")
    summed = jnp.einsum("cka,kcjb->jab", integrals, amplitudes, preferred_element_type=F32)
    pairs, virt, cols = summed.shape
    own_pairs, own_rows = pairs // ka_size, virt // tile_size
    ka_bits, tile_bits = bits_of(ka_size), bits_of(tile_size)
    grid = summed.reshape([2] * len(ka_bits) + [own_pairs] + [2] * len(tile_bits) + [own_rows, cols])
    for i, bit in enumerate(ka_bits):
        grid = trade(grid, "ka", bit, len(ka_bits) - 1 - i, F32)
    for i, bit in enumerate(tile_bits):
        grid = trade(grid, "tile", bit, len(tile_bits) - i, F32)
    tile_pos, ka_pos = lax.axis_index("tile"), lax.axis_index("ka")
    own_virt = lax.dynamic_slice_in_dim(virt_energy, tile_pos * own_rows, own_rows, 0)
    own_e = lax.dynamic_slice_in_dim(pair_energy, ka_pos * own_pairs, own_pairs, 0)
    denominator = own_virt[None, :, None] + virt_energy[None, None, :] - own_e[:, None, None]
    return (grid / denominator).astype(BF16)


def solution(mesh):
    fits = mesh.shape["ka"] == 4 and mesh.shape["tile"] == 8

    def per_device(integrals, amplitudes, virt_energy, pair_energy):
        own_rows = integrals.shape[2] // lax.axis_size("tile")
        depth = amplitudes.shape[0] * amplitudes.shape[1]
        plain = fits and own_rows % 16 == 0 and depth % 960 == 0 and amplitudes.shape[2] == 8
        plain = plain and integrals.shape[2] % 128 == 0 and depth // 128 >= integrals.shape[2] // 128
        plan = on_chip_plan if plain else any_plan
        return plan(integrals, amplitudes, virt_energy, pair_energy)

    in_specs = (P("tile", "ka", None), P("ka", "tile", None, None), P(), P())
    out_specs = P("ka", "tile", None)
    return jax.shard_map(
        per_device, mesh=mesh, in_specs=in_specs, out_specs=out_specs, check_vma=False
    )
```

```python
import functools

import jax
import jax.numpy as jnp
from jax import lax
from jax.experimental import pallas as pl
from jax.experimental.pallas import tpu as pltpu
from jax.sharding import PartitionSpec as P

F32, BF16 = jnp.float32, jnp.bfloat16
SPAN, BASE = 248.0, 124.0
EDGE = 16
LONG = 1 << 35
PAD = 8
FAR = pl.BlockSpec(memory_space=pltpu.HBM)
WHOLE = pl.BlockSpec(memory_space=pltpu.VMEM)
SCALAR = pl.BlockSpec(memory_space=pltpu.SMEM)


def shape(dims, dtype):
    return jax.ShapeDtypeStruct(tuple(dims), dtype)


def encode(out_ref, value):
    rows, cols = value.shape
    tall = value.reshape(rows // 8, 8, cols)
    size = jnp.abs(tall)
    top = jnp.maximum(jnp.max(size, axis=0) * 1.01, 1e-30).astype(BF16)
    factor = SPAN / top.astype(F32)
    code = jnp.exp2(size * factor[None] - BASE)
    code = jnp.where(tall < 0, -code, code)
    out_ref[pl.ds(0, rows), :] = code.reshape(rows, cols).astype(BF16)
    out_ref[pl.ds(rows, PAD), :] = top


def decode(ref, first, rows):
    total, cols = ref.shape[0] - PAD, ref.shape[1]
    factor = ref[pl.ds(total, PAD), :].astype(F32) * (1.0 / SPAN)
    code = ref[pl.ds(first, rows), :].astype(F32).reshape(rows // 8, 8, cols)
    size = (jnp.log2(jnp.abs(code)) + BASE) * factor[None]
    return jnp.where(code < 0, -size, size).reshape(rows, cols)


def call(kernel, outs, *args, specs=None, room=12, scratch=(), alias=None, after=(), work=1000, out_specs=None):
    specs = list(specs or [WHOLE] * len(args))
    count = len(after)

    def body(*refs):
        kernel(*refs[count:])

    return pl.pallas_call(
        body,
        in_specs=[pl.BlockSpec(memory_space=pl.ANY)] * count + specs,
        out_specs=out_specs or [WHOLE] * len(outs),
        out_shape=outs,
        scratch_shapes=scratch,
        input_output_aliases={i + count: o for i, o in (alias or {}).items()},
        compiler_params=pltpu.CompilerParams(vmem_limit_bytes=room << 20),
        cost_estimate=pl.CostEstimate(
            flops=work, bytes_accessed=1000, transcendentals=0
        ),
    )(*after, *args)


def plane(flat, group, side, rows=slice(None)):
    cols = flat.shape[2] // 2
    return flat.at[group, rows, pl.ds(pl.multiple_of(side * cols, 128), cols)]


def home_planes(place):
    x, core = place[0], place[1]
    return (2 * core, x), (2 * core + 1, 0), (2 * core + 1, 1), (2 * core, 1 - x)


def front_kernel(place, wide, amp, turned, out, flat, far, held, sem, far_sem, *, block, far_block, unit, own_rows, tiles_y, tiles_z):
    depth, pairs, cols = amp.shape
    virt = wide.shape[1]
    copies = [
        pltpu.make_async_copy(amp.at[pl.ds(at, block)], held.at[pl.ds(at, block)], sem.at[at // block])
        for at in range(0, depth, block)
    ]
    for copy in copies:
        copy.start()
    bulk = own_rows - EDGE

    def turn(first, count):
        t = wide[:, first : first + count].T
        for at in range(0, count, EDGE):
            tile, row = divmod(first + at, own_rows)
            z, y = divmod(tile, tiles_y)
            if row < bulk:
                to = (y * tiles_z + z) * bulk + row
            else:
                to = tiles_y * tiles_z * bulk + (z * tiles_y + y) * EDGE
            turned[to : to + EDGE, :] = t[at : at + EDGE]

    leaving = []
    n = unit * pairs
    r = lax.broadcasted_iota(jnp.int32, (n, n), 0)
    c = lax.broadcasted_iota(jnp.int32, (n, n), 1)
    perm = (c == (r % unit) * pairs + r // unit).astype(F32).astype(BF16)
    for at in range(0, depth, unit):
        if at % block == 0:
            copies[at // block].wait()
        part = held[at : at + unit].reshape(n, cols)
        moved = jnp.dot(perm, part, preferred_element_type=F32).astype(BF16)
        for j in range(pairs):
            flat[j % 4, at : at + unit, pl.ds(j // 4 * cols, cols)] = moved[j * unit : (j + 1) * unit]
        if at // unit % 4 == 2 and at // unit // 4 < virt // 128:
            turn(at // unit // 4 * 128, 128)
        done = at + unit
        if done % far_block == 0:
            here = pl.ds(done - far_block, far_block)
            for slot, (group, side) in enumerate(home_planes(place)):
                copy = pltpu.make_async_copy(
                    plane(flat, group, side, here), far.at[slot, here], far_sem.at[slot, done // far_block - 1]
                )
                copy.start()
                leaving.append(copy)
    x, core = place[0], place[1]
    rows = tiles_y * tiles_z * bulk
    out[...] = jnp.dot(
        turned[pl.ds(0, rows), :], plane(flat, 2 * (1 - core), 1 - x)[...], preferred_element_type=F32
    )
    for copy in leaving:
        copy.wait()


def product_kernel(place, turned, flat, *outs, jobs, bulk, tiles_y, tiles_z):
    x, core, y = place[0], place[1], place[2]
    rows = tiles_z * bulk

    cols = flat.shape[2] // 2

    def dot(at, height, group, side=None):
        rhs = flat.at[group] if side is None else plane(flat, group, side)
        return jnp.dot(turned[pl.ds(at, height), :], rhs[...], preferred_element_type=F32)

    for out, parts in zip(outs[:-1], jobs):
        base = 0
        for who, part in parts:
            pair = 2 * (core if who == "own" else 1 - core)
            if part == "a_away":
                out[pl.ds(base, 2 * rows), :] = dot(0, 2 * rows, pair, 1 - x)
            elif part == "a_home":
                out[pl.ds(base, 2 * rows), :] = dot(0, 2 * rows, pair, x)
            elif part in ("b_away", "b_home"):
                side = y if part == "b_home" else 1 - y
                got = dot(pl.multiple_of(side * rows, 16), rows, pair + 1)
                for xx in range(2):
                    out[pl.ds(base + xx * rows, rows), :] = got[:, xx * cols :][:, :cols]
            else:
                for i in range(2):
                    wide = dot(2 * rows, tiles_y * tiles_z * EDGE, pair + i)
                    for xx in range(2):
                        got = wide[:, xx * cols :][:, :cols]
                        for zz in range(tiles_z):
                            for yy in range(tiles_y):
                                at = base + (((zz * tiles_y + yy) * 2 + xx) * 2 + i) * EDGE
                                out[pl.ds(at, EDGE), :] = got[(zz * tiles_y + yy) * EDGE :][:EDGE]
            base += 2 * rows if part != "c" else 4 * tiles_y * tiles_z * EDGE


def home_kernel(place, turned, far, core_a, core_b, out_a, out_b, held, sem, *, bulk, tiles_z):
    y = place[2]
    rows = tiles_z * bulk
    copies = [pltpu.make_async_copy(far.at[slot], held.at[slot], sem.at[slot]) for slot in range(3)]
    for copy in copies:
        copy.start()

    def dot(at, height, slot):
        return jnp.dot(turned[pl.ds(at, height), :], held[slot], preferred_element_type=F32)

    copies[0].wait()
    out_a[...] = core_a[...] + dot(0, 2 * rows, 0)
    for xx in range(2):
        copies[1 + xx].wait()
        here = pl.ds(xx * rows, rows)
        out_b[here, :] = core_b[here, :] + dot(pl.multiple_of(y * rows, 16), rows, 1 + xx)


def edge_kernel(place, turned, far, out, held, sem, *, first, tiles_y, tiles_z):
    x = place[0]
    copies = [pltpu.make_async_copy(far.at[slot], held.at[slot], sem.at[slot]) for slot in range(4)]
    for copy in copies:
        copy.start()
    for slot, (xx, i) in enumerate(((x, 0), (0, 1), (1, 1), (1 - x, 0))):
        copies[slot].wait()
        got = jnp.dot(
            turned[pl.ds(first, tiles_y * tiles_z * EDGE), :], held[slot], preferred_element_type=F32
        )
        for z in range(tiles_z):
            for y in range(tiles_y):
                at = pl.multiple_of((((z * tiles_y + y) * 2 + xx) * 2 + i) * EDGE, EDGE)
                out[pl.ds(at, EDGE), :] = got[(z * tiles_y + y) * EDGE :][:EDGE]


def first_kernel(own, core, out):
    encode(out, own[...] + core[pl.ds(0, own.shape[0]), :])


def spread_kernel(place, own, core, keep, *outs, rows, count, base):
    z = place[3]

    def total(to):
        at = pl.multiple_of(to * rows, 16)
        return own[pl.ds(at, rows), :] + core[pl.ds(base + at, rows), :]

    for hop in range(1, count):
        encode(outs[hop - 1], total(z ^ hop))
    keep[...] = total(z)


def part_of(own, gots, to, rows):
    at = pl.multiple_of(to * rows, 16)
    value = own[pl.ds(at, rows), :]
    for got in gots:
        value = value + decode(got, at, rows)
    return value


def halve_kernel(place, own, *refs, which, rows):
    *gots, keep, out = refs
    encode(out, part_of(own, gots, 1 - place[which], rows))
    keep[...] = part_of(own, gots, place[which], rows)


def away_kernel(place, own, got, out, *, which, rows):
    encode(out, part_of(own, [got], 1 - place[which], rows))


def stay_kernel(place, own_a, got_a, own_b, got_b, keep_a, keep_b, *, which_a, which_b, rows):
    keep_a[...] = part_of(own_a, [got_a], place[which_a], rows)
    keep_b[...] = part_of(own_b, [got_b], place[which_b], rows)


def line_kernel(place, keep_a, got_a, keep_b, got_b, *outs, rows, hops):
    for hop, out in zip(hops, outs):
        first = part_of(keep_a, [got_a], place[3] ^ hop, rows)
        second = part_of(keep_b, [got_b], place[3] ^ hop, rows)
        value = jnp.concatenate([first, second], 0)
        if hop:
            encode(out, value)
        else:
            out[...] = value


def rest_kernel(place, keep_a, got_a, keep_b, got_b, row_e, col_e, pair_e, own, below, *, rows):
    line_kernel(place, keep_a, got_a, keep_b, got_b, own, rows=rows, hops=[0])
    for i in range(below.shape[0]):
        below[i] = row_e[...] + col_e[...] - pair_e[i]


def bulk_kernel(own, *refs):
    gots, (below, out) = refs[:-2], refs[-2:]
    value = own[...]
    for got in gots:
        value = value + decode(got, 0, own.shape[0])
    bulk = own.shape[0] // below.shape[0]
    for i in range(below.shape[0]):
        here = pl.ds(i * bulk, bulk)
        out[here, :] = (value[i * bulk : (i + 1) * bulk] / below[i, :bulk]).astype(BF16)


def last_kernel(bulk_rows, keep_c, got_c, below, out):
    edge = keep_c[...] + decode(got_c, 0, keep_c.shape[0])
    bulk = out.shape[1] - EDGE
    for i in range(out.shape[0]):
        out[i, pl.ds(0, bulk), :] = bulk_rows[pl.ds(i * bulk, bulk), :]
        out[i, pl.ds(bulk, EDGE), :] = (edge[i * EDGE : (i + 1) * EDGE] / below[i, bulk:]).astype(BF16)


def swap(value, axis, bit):
    return lax.ppermute(value, axis, [(i, i ^ bit) for i in range(lax.axis_size(axis))])


def on_chip_plan(integrals, amplitudes, virt_energy, pair_energy):
    tile_size, ka_size = lax.axis_size("tile"), lax.axis_size("ka")
    tile_pos, ka_pos = lax.axis_index("tile"), lax.axis_index("ka")
    k, c, pairs, cols = amplitudes.shape
    depth, virt = k * c, integrals.shape[2]
    own_pairs, own_rows = pairs // ka_size, virt // tile_size
    tiles_y, tiles_z = 2, tile_size // 2
    hops = [2, 1] + [hop for hop in range(3, tiles_z)]
    bulk = own_rows - EDGE
    rows = bulk * tiles_z
    edges = EDGE * tiles_y * own_pairs * 2
    place = jnp.stack([ka_pos // 2, ka_pos % 2, tile_pos % 2, tile_pos // 2]).astype(jnp.int32)
    wide = integrals.transpose(1, 0, 2).reshape(depth, virt)

    def full(height):
        return shape((height, cols), F32)

    def coded(height):
        return shape((height + PAD, cols), BF16)

    block, far_block = 320, 160
    held = pltpu.VMEM((pairs // 2, depth, 2 * cols), BF16)
    turned, c_a, flat, far = call(
        functools.partial(
            front_kernel, block=block, far_block=far_block, unit=32, own_rows=own_rows, tiles_y=tiles_y, tiles_z=tiles_z
        ),
        [pltpu.VMEM((virt, depth), BF16), full(2 * rows), held, pltpu.HBM((4, depth, cols), BF16)],
        place, wide, amplitudes.reshape(depth, pairs, cols), specs=[SCALAR, WHOLE, FAR], room=40, out_specs=[WHOLE] * 3 + [FAR],
        scratch=[
            pltpu.VMEM((depth, pairs, cols), BF16),
            pltpu.SemaphoreType.DMA((depth // block,)),
            pltpu.SemaphoreType.DMA((4, depth // far_block)),
        ],
    )

    def products(flat, *jobs, after=()):
        heights = {"a": 2 * rows, "b": 2 * rows, "c": tiles_z * edges}
        outs = [full(sum(heights[part[0]] for _, part in parts)) for parts in jobs]
        return call(
            functools.partial(product_kernel, jobs=jobs, bulk=bulk, tiles_y=tiles_y, tiles_z=tiles_z),
            outs + [held], place, turned, flat,
            specs=[SCALAR, WHOLE, WHOLE], alias={2: len(jobs)}, after=after,
        )

    g_a = swap(c_a, "ka", 1)
    c_b, c_c, flat = products(flat, [("core", "b_away")], [("core", "c")])
    g_b, g_c = swap(c_b, "ka", 1), swap(c_c, "ka", 1)
    c_ah, c_bh, flat = products(flat, [("core", "a_home")], [("core", "b_home")])
    g_ah, g_bh = swap(c_ah, "ka", 1), swap(c_bh, "ka", 1)
    o_a, o_b, flat = products(flat, *([("own", part)] for part in ("a_away", "b_away")))
    (send_a,) = call(first_kernel, [coded(2 * rows)], o_a, g_a)
    got_a = swap(send_a, "ka", 2)
    (send_b,) = call(first_kernel, [coded(2 * rows)], o_b, g_b, after=[send_a])
    got_b = swap(send_b, "tile", 1)
    (o_c,) = call(
        functools.partial(edge_kernel, first=2 * rows, tiles_y=tiles_y, tiles_z=tiles_z),
        [full(tiles_z * edges)], place, turned, far, specs=[SCALAR, WHOLE, FAR], after=[send_b], room=16,
        scratch=[pltpu.VMEM((4, depth, cols), BF16), pltpu.SemaphoreType.DMA((4,))],
    )
    keep_c, *sends = call(
        functools.partial(spread_kernel, rows=edges, count=tiles_z, base=0),
        [full(edges)] + [coded(edges)] * (tiles_z - 1), place, o_c, g_c,
        specs=[SCALAR, WHOLE, WHOLE], after=[send_b],
    )
    gots_c = [swap(sends[hop - 1], "tile", 2 * hop) for hop in hops]

    h_a, h_b = call(
        functools.partial(home_kernel, bulk=bulk, tiles_z=tiles_z), [full(2 * rows), full(2 * rows)],
        place, turned, far, g_ah, g_bh, specs=[SCALAR, WHOLE, FAR, WHOLE, WHOLE], after=[keep_c], room=16,
        scratch=[pltpu.VMEM((3, depth, cols), BF16), pltpu.SemaphoreType.DMA((3,))],
    )
    away = functools.partial(away_kernel, rows=rows)
    specs = [SCALAR, WHOLE, WHOLE]
    (send_a,) = call(functools.partial(away, which=2), [coded(rows)], place, h_a, got_a, specs=specs)
    (send_b,) = call(
        functools.partial(away, which=0), [coded(rows)], place, h_b, got_b, specs=specs, after=[send_a]
    )
    keep_a, keep_b = call(
        functools.partial(stay_kernel, which_a=2, which_b=0, rows=rows), [full(rows)] * 2,
        place, h_a, got_a, h_b, got_b, specs=[SCALAR] + [WHOLE] * 4, after=[send_b],
    )
    got_a = swap(send_a, "tile", 1)
    got_b = swap(send_b, "ka", 2)
    keep_c, send_c = call(
        functools.partial(halve_kernel, which=2, rows=edges // 2), [full(edges // 2), coded(edges // 2)],
        place, keep_c, *gots_c, specs=[SCALAR] + [WHOLE] * tiles_z, work=LONG, after=[keep_a],
    )
    got_c = swap(send_c, "tile", 1)

    height = own_pairs * bulk
    line = functools.partial(line_kernel, rows=bulk)
    specs = [SCALAR] + [WHOLE] * 4
    sends = call(
        functools.partial(line, hops=hops), [coded(height)] * len(hops),
        place, keep_a, got_a, keep_b, got_b, specs=specs, after=[send_c],
    )
    gots = [swap(send, "tile", 2 * hop) for hop, send in zip(hops, sends)]
    keep_c, send_c = call(
        functools.partial(halve_kernel, which=0, rows=edges // 4), [full(edges // 4), coded(edges // 4)],
        place, keep_c, got_c, specs=[SCALAR, WHOLE, WHOLE], after=[sends[0]],
    )
    got_c = swap(send_c, "ka", 2)
    own_virt = lax.dynamic_slice_in_dim(virt_energy, tile_pos * own_rows, own_rows, 0)
    own_e = lax.dynamic_slice_in_dim(pair_energy, ka_pos * own_pairs, own_pairs, 0)
    own, below = call(
        functools.partial(rest_kernel, rows=bulk), [full(height), shape((own_pairs, own_rows, cols), F32)],
        place, keep_a, got_a, keep_b, got_b, own_virt[:, None], virt_energy[None, :], own_e,
        specs=specs + [WHOLE, WHOLE, SCALAR], after=[keep_c],
    )
    (bulk_rows,) = call(bulk_kernel, [shape((height, cols), BF16)], own, *gots, below)
    (out,) = call(last_kernel, [shape((own_pairs, own_rows, cols), BF16)], bulk_rows, keep_c, got_c, below)
    return out


def trade(parts, axis, bit, dim, wire):
    mine = (lax.axis_index(axis) // bit) % 2
    keep = lax.dynamic_index_in_dim(parts, mine, dim, keepdims=False)
    away = lax.dynamic_index_in_dim(parts, 1 - mine, dim, keepdims=False)
    got = swap(away.astype(wire), axis, bit)
    return keep + got.astype(F32)


def bits_of(size):
    return [1 << i for i in range(size.bit_length() - 1)]


def any_plan(integrals, amplitudes, virt_energy, pair_energy):
    tile_size, ka_size = lax.axis_size("tile"), lax.axis_size("ka")
    summed = jnp.einsum("cka,kcjb->jab", integrals, amplitudes, preferred_element_type=F32)
    pairs, virt, cols = summed.shape
    own_pairs, own_rows = pairs // ka_size, virt // tile_size
    ka_bits, tile_bits = bits_of(ka_size), bits_of(tile_size)
    grid = summed.reshape([2] * len(ka_bits) + [own_pairs] + [2] * len(tile_bits) + [own_rows, cols])
    for i, bit in enumerate(ka_bits):
        grid = trade(grid, "ka", bit, len(ka_bits) - 1 - i, F32)
    for i, bit in enumerate(tile_bits):
        grid = trade(grid, "tile", bit, len(tile_bits) - i, F32)
    tile_pos, ka_pos = lax.axis_index("tile"), lax.axis_index("ka")
    own_virt = lax.dynamic_slice_in_dim(virt_energy, tile_pos * own_rows, own_rows, 0)
    own_e = lax.dynamic_slice_in_dim(pair_energy, ka_pos * own_pairs, own_pairs, 0)
    denominator = own_virt[None, :, None] + virt_energy[None, None, :] - own_e[:, None, None]
    return (grid / denominator).astype(BF16)


def solution(mesh):
    fits = mesh.shape["ka"] == 4 and mesh.shape["tile"] == 8

    def per_device(integrals, amplitudes, virt_energy, pair_energy):
        own_rows = integrals.shape[2] // lax.axis_size("tile")
        depth = amplitudes.shape[0] * amplitudes.shape[1]
        plain = fits and own_rows % 16 == 0 and depth % 960 == 0 and amplitudes.shape[2] == 8
        plain = plain and integrals.shape[2] % 128 == 0 and depth // 128 >= integrals.shape[2] // 128
        plan = on_chip_plan if plain else any_plan
        return plan(integrals, amplitudes, virt_energy, pair_energy)

    in_specs = (P("tile", "ka", None), P("ka", "tile", None, None), P(), P())
    out_specs = P("ka", "tile", None)
    return jax.shard_map(
        per_device, mesh=mesh, in_specs=in_specs, out_specs=out_specs, check_vma=False
    )
```
